256 devices in a mesh: prow: 8 (over z), pcol: 32 (over x, y, core).
Axes of the slice: x: 4, y: 4, z: 8, core: 2. Of those that a mesh axis runs over, the one named last changes fastest.
Arguments:
- kernel: float32 [8, 8, 256, 2, 32, 256], P(None, 'prow', None, None, 'pcol'), may hold values from 0 to 1.5, as said below
- pivots: int32 [2], replicated, may hold values from 0 to 63, as said below
Outputs:
- panels: float32 [2, 8, 8, 256, 256], P(None, None, 'prow')
- trailing: float32 [8, 8, 256, 2, 32, 256], P(None, 'prow', None, None, 'pcol')
The draws below stay inside these ranges and needn't reach their ends.
Inputs may be any that keep to these rules, and one draw needn't show every extreme that they name: `kernel`: symmetric; a positive semidefinite matrix plus 0.5 times the identity. `pivots`: two different block numbers; one of them is the newest block, 63, in either position.
All inputs are finite; a program needn't handle non-finite values.
Results may differ from the reference program's by a relative error of at most 0.0003.
Values sent between devices are 32-bit elements; how exact they have to be, the bound alone decides.
No kernel may reach another device: no remote copies, remote signals or barrier semaphores. Data moves between devices by JAX's collectives and lax.ppermute only.
A program may use at most 64 MiB of HBM per device.

```python
import jax
import jax.numpy as jnp
from jax import lax

M = 16384
NB = 256
F_DESC = 8
NBLK = 64
BR = 8
BC = 2
N_PROW = 8
N_PCOL = 32


KERNEL_SCALE = 8.0


RIDGE = 0.5


def draw_kernel(key, part):
    first_key = jax.random.fold_in(jax.random.fold_in(key, 7), 0)
    descriptors = jax.random.normal(first_key, (M, F_DESC), jnp.float32)
    column_numbers = jnp.arange(M, dtype=jnp.int32)

    def kernel_rows(start):
        segment = lax.dynamic_slice_in_dim(descriptors, start, NB, 0)
        distance = jnp.sum((segment[:, None, :] - descriptors[None, :, :]) ** 2, axis=2)
        diagonal = (start + jnp.arange(NB, dtype=jnp.int32))[:, None] == column_numbers[None, :]
        return jnp.exp(-distance / KERNEL_SCALE) + jnp.where(diagonal, RIDGE, 0.0)
    starts = jnp.arange(NBLK, dtype=jnp.int32) * NB
    values = lax.map(kernel_rows, starts)
    return values.reshape(BR, NBLK // BR, NB, BC, NBLK // BC, NB).astype(jnp.float32)


def draw_pivots(key, part):
    other_key, order_key = jax.random.split(jax.random.fold_in(key, 3))
    other = jax.random.randint(other_key, (), 0, NBLK - 1, dtype=jnp.int32)
    newest = jnp.full((), NBLK - 1, dtype=jnp.int32)
    flipped = jax.random.randint(order_key, (), 0, 2, dtype=jnp.int32) == 1
    first = jnp.where(flipped, other, newest)
    second = jnp.where(flipped, newest, other)
    return jnp.stack([first, second]).astype(jnp.int32)


def setup_inputs(seed: int = 0) -> dict:
    key_of = jax.random.split(jax.random.key(seed), 3)
    kernel = draw_kernel(jax.random.fold_in(key_of[2], 71), 0)
    pivots = draw_pivots(jax.random.fold_in(key_of[2], 71), 0)
    return {"kernel": kernel, "pivots": pivots}


HIGHEST = lax.Precision.HIGHEST

def pivot_step(matrix, pivot_block):
    start_row = (pivot_block * NB).astype(jnp.int32)
    column = lax.dynamic_slice_in_dim(matrix, start_row, NB, 1)
    diagonal = lax.dynamic_slice_in_dim(column, start_row, NB, 0)
    identity = jnp.eye(NB, dtype=jnp.float32)
    factor = jnp.linalg.cholesky(diagonal)
    inverse = lax.linalg.triangular_solve(factor, identity, left_side=True, lower=True)
    panel_rows = jnp.dot(column.astype(jnp.float32), inverse.T.astype(jnp.float32), precision=HIGHEST, preferred_element_type=jnp.float32)
    matrix = matrix - jnp.dot(panel_rows.astype(jnp.float32), panel_rows.T.astype(jnp.float32), precision=HIGHEST, preferred_element_type=jnp.float32)
    block_ids = (jnp.arange(M, dtype=jnp.int32) // NB).astype(jnp.int32)
    retained = block_ids != pivot_block.astype(jnp.int32)
    matrix = jnp.where(retained[:, None] & retained[None, :], matrix, jnp.zeros((), jnp.float32))
    return (panel_rows, matrix)

def reference(kernel, pivots):
    matrix = kernel.reshape(M, M)
    first_rows, matrix = pivot_step(matrix, pivots[0])
    second_rows, matrix = pivot_step(matrix, pivots[1])
    panels = jnp.stack([first_rows, second_rows]).reshape(2, BR, N_PROW, NB, NB)
    trailing = matrix.reshape(BR, N_PROW, NB, BC, N_PCOL, NB)
    return (panels, trailing)
```

```python
import jax
import jax.numpy as jnp
from jax import lax
from jax.experimental import pallas as pl
from jax.experimental.pallas import tpu as pltpu
from jax.sharding import PartitionSpec as P

BASE = 64
GROUP = 8

def split(v):
    high = v.astype(jnp.bfloat16)
    low = (v - high.astype(jnp.float32)).astype(jnp.bfloat16)
    return high, low

def product(a, b, dims):
    ah, al = split(a)
    bh, bl = split(b)
    f = lambda u, v: lax.dot_general(u, v, (dims, ((), ())), preferred_element_type=jnp.float32)
    return f(ah, bh) + (f(ah, bl) + f(al, bh))

def mm_nt(a, b):
    return product(a, b, ((1,), (1,)))

def mm(a, b):
    return product(a, b, ((1,), (0,)))

def factor_group(scalars):
    n = GROUP
    g = [row[:] for row in scalars]
    unit = [[None] * n for _ in range(n)]
    pivots = []
    inverses = []
    for q in range(n):
        d = g[q][q]
        inv = 1.0 / d
        pivots.append(d)
        inverses.append(inv)
        for i in range(q + 1, n):
            unit[i][q] = g[i][q] * inv
        for i in range(q + 1, n):
            for k in range(q + 1, i + 1):
                g[i][k] = g[i][k] - unit[i][q] * g[k][q]
    w = [[None] * n for _ in range(n)]
    for q in range(n):
        for i in range(q + 1, n):
            acc = unit[i][q]
            for k in range(q + 1, i):
                acc = acc + unit[i][k] * w[k][q]
            w[i][q] = -acc
    return w, pivots, inverses

def base_inverse(s):
    lanes = 2 * BASE
    row = lax.broadcasted_iota(jnp.int32, (BASE, BASE), 0)
    col = lax.broadcasted_iota(jnp.int32, (BASE, BASE), 1)
    eye = jnp.where(row == col, 1.0, 0.0).astype(jnp.float32)
    table = jnp.concatenate([s, eye], axis=1)
    groups = [table[GROUP * h : GROUP * h + GROUP, :] for h in range(BASE // GROUP)]
    shape = (GROUP, lanes)
    sub = lax.broadcasted_iota(jnp.int32, shape, 0)
    spread = lambda v: jnp.broadcast_to(v, shape)
    done = []
    for g in range(BASE // GROUP):
        p = groups[g]
        start = GROUP * g
        cols = [spread(p[:, start + q : start + q + 1]) for q in range(GROUP)]
        scalars = [[spread(cols[q][i : i + 1, :]) if i >= q else None for q in range(GROUP)] for i in range(GROUP)]
        w, pivots, inverses = factor_group(scalars)
        rows = [spread(p[q : q + 1, :]) for q in range(GROUP)]
        reduced = []
        for i in range(GROUP):
            acc = rows[i]
            for q in range(i):
                acc = acc + w[i][q] * rows[q]
            reduced.append(acc)
        for h in range(g + 1, BASE // GROUP):
            t = groups[h]
            cb = [spread(t[:, start + q : start + q + 1]) for q in range(GROUP)]
            for q in range(GROUP):
                v = cb[q]
                for k in range(q):
                    v = v + w[q][k] * cb[k]
                t = t - (v * inverses[q]) * reduced[q]
            groups[h] = t
        out = jnp.zeros(shape, jnp.float32)
        for q in range(GROUP):
            out = jnp.where(sub == q, reduced[q] * lax.rsqrt(pivots[q]), out)
        done.append(out)
    return jnp.concatenate(done, axis=0)[:, BASE:]

def chain_kernel(d_ref, m_ref, s_ref):
    n = d_ref.shape[0]
    s_ref[...] = d_ref[...]
    m_ref[...] = jnp.zeros_like(m_ref)
    def solve(at, size):
        if size == BASE:
            m_ref[at : at + size, at : at + size] = base_inverse(s_ref[at : at + size, at : at + size])
            return
        half = size // 2
        lo, mid, hi = slice(at, at + half), slice(at + half, at + size), None
        solve(at, half)
        m0 = m_ref[lo, lo]
        below = mm_nt(s_ref[mid, lo], m0)
        s_ref[mid, mid] = s_ref[mid, mid] - mm_nt(below, below)
        w = mm(below, m0)
        solve(at + half, half)
        m_ref[mid, lo] = -mm(m_ref[mid, mid], w)
    solve(0, n)

def chain(d):
    n = d.shape[0]
    return pl.pallas_call(
        chain_kernel,
        out_shape=jax.ShapeDtypeStruct((n, n), jnp.float32),
        in_specs=[pl.BlockSpec(memory_space=pltpu.VMEM)],
        out_specs=pl.BlockSpec(memory_space=pltpu.VMEM),
        scratch_shapes=[pltpu.VMEM((n, n), jnp.float32)],
        compiler_params=pltpu.CompilerParams(vmem_limit_bytes=32 * 1024 * 1024),
    )(d)


AXES = ("prow", "pcol")
NB = 256
NEWEST = 63


def shards(kernel, pivots):
    height, width = lax.axis_size("prow"), lax.axis_size("pcol")
    assert (height, width) == (8, 32)
    br, bc = kernel.shape[0], kernel.shape[3]
    matrix = kernel.reshape(br, NB, bc, NB)
    r = lax.axis_index("prow")
    c = lax.axis_index("pcol")
    flipped = pivots[0] == NEWEST
    other = jnp.where(flipped, pivots[1], pivots[0])
    root_row, root_col, root_t = other % height, other % width, other // width
    device = lambda row, column: row * width + column
    everyone = [(row, column) for row in range(height) for column in range(width)]
    gate = lambda value, *after: lax.optimization_barrier((value, *after))[0]

    chunk = 2 * NB // height
    per_root = height // 2
    other_rows = lax.dynamic_index_in_dim(matrix, other // height, 0, keepdims=False).reshape(NB, bc * NB)
    newest_rows = matrix[NEWEST // height].reshape(NB, bc * NB)
    take = lambda rows, m: rows[m * chunk : (m + 1) * chunk]

    def scatter_from(root):
        def run(other_rows, newest_rows):
            total = None
            for m in range(per_root):
                pair = [(device(root, k), device(m, k)) for k in range(width)]
                last = [(device(height - 1, k), device(per_root + m, k)) for k in range(width)]
                a, b = take(other_rows, m), take(newest_rows, m)
                if root == height - 1:
                    parts = [lax.ppermute(a, AXES, pair), lax.ppermute(b, AXES, last)]
                else:
                    parts = [lax.ppermute(jnp.where(r == height - 1, b, a), AXES, pair + last)]
                for part in parts:
                    total = part if total is None else total + part
            return total
        return run

    piece = lax.switch(root_row, [scatter_from(root) for root in range(height)], other_rows, newest_rows)

    swap = [(device(row, 8 * (col // 8) + k), device(k, 8 * (col // 8) + row)) for row in range(height) for col in range(0, width, 8) for k in range(8)]
    moved = lax.ppermute(piece, AXES, swap)
    gathered = lax.all_gather(moved, "pcol", axis=0, tiled=False)

    left = lax.dynamic_slice_in_dim(piece, root_t * NB, NB, 1)
    right = piece[:, NB:]
    core, ypos, xpos = c % 2, (c // 2) % 4, c // 8
    rcore, ry, rx = root_col % 2, (root_col // 2) % 4, root_col // 8
    both = jnp.concatenate([left, right], axis=1)
    side = lax.broadcasted_iota(jnp.int32, (chunk, 2 * NB), 1) < NB
    got = lax.ppermute(both, AXES, [(device(a, b), device(a, b ^ 1)) for a, b in everyone])
    both = jnp.where(jnp.where(side, core == rcore, core == 1), both, got)
    half = chunk // 2
    mine = lax.dynamic_slice_in_dim(both, core * half, half, 0)
    side = side[:half]

    def spread(value, position, goal, last, shift):
        parts = [value]
        for d in range(1, 4):
            parts.append(lax.ppermute(value, AXES, [(device(a, b), device(a, shift(b, d))) for a, b in everyone]))
        source_left, source_right = (position - goal) % 4, (position - last) % 4
        source = jnp.where(side, source_left, source_right)
        out = parts[0]
        for d in range(1, 4):
            out = jnp.where(source == d, parts[d], out)
        return out

    mine = spread(mine, xpos, rx, 3, lambda b, d: (b + 8 * d) % 32)
    mine = spread(mine, ypos, ry, 3, lambda b, d: (b // 8) * 8 + (b + 2 * d) % 8)
    around = [lax.ppermute(mine, AXES, [(device(a, b), device((a + d) % height, b)) for a, b in everyone]) for d in range(7, 0, -1)]
    ring = jnp.stack(around + [mine])
    ring = lax.dynamic_slice_in_dim(jnp.concatenate([ring, ring]), 7 - r, height, 0)
    twin = lax.ppermute(ring, AXES, [(device(a, b), device(a, b ^ 1)) for a, b in everyone])
    low, high = jnp.where(core == 0, ring, twin), jnp.where(core == 0, twin, ring)
    diagonal = jnp.stack([low, high], axis=1).reshape(2 * NB, 2 * NB)
    swapped = jnp.roll(diagonal, (NB, NB), (0, 1))
    inverse = chain(jnp.where(flipped, swapped, diagonal))
    weights = inverse.T
    weights = jnp.where(flipped, jnp.roll(weights, NB, 0), weights)

    piece = gate(piece, mine)
    around = [lax.ppermute(piece, AXES, [(device(a, b), device((a + d) % height, b)) for a, b in everyone]) for d in range(7, 0, -1)]
    ring = jnp.stack(around + [piece])
    crossing = lax.dynamic_slice_in_dim(jnp.concatenate([ring, ring]), 7 - r, height, 0).reshape(2 * NB, bc * NB)

    columns = gathered.reshape(bc * 2, 8, chunk, bc, NB)
    columns = columns.transpose(3, 0, 4, 1, 2).reshape(br * NB, 2 * NB)
    dot = lambda a, b, dims: lax.dot_general(a, b, (dims, ((), ())), precision=lax.Precision.HIGHEST, preferred_element_type=jnp.float32)
    rows = dot(columns, weights, ((1,), (0,)))
    cross = dot(weights, crossing, ((0,), (0,)))
    product = dot(rows, cross, ((1,), (0,))).reshape(br, NB, bc, NB)
    row_block = jnp.arange(br) * height + r
    col_block = jnp.arange(bc) * width + c
    keep_row = (row_block != pivots[0]) & (row_block != pivots[1])
    keep_col = (col_block != pivots[0]) & (col_block != pivots[1])
    keep = keep_row[:, None, None, None] & keep_col[None, None, :, None]
    trailing = jnp.where(keep, matrix - product, 0.0)
    rows = rows.reshape(br, NB, 2, NB)
    second = jnp.where((row_block != pivots[0])[:, None, None], rows[:, :, 1], 0.0)
    panels = jnp.stack([rows[:, :, 0], second])[:, :, None]
    return panels, trailing.reshape(kernel.shape)


def solution(mesh):
    in_specs = (P(None, "prow", None, None, "pcol", None), P())
    out_specs = (P(None, None, "prow", None, None), P(None, "prow", None, None, "pcol", None))
    return jax.shard_map(shards, mesh=mesh, in_specs=in_specs, out_specs=out_specs, check_vma=False)
```

```python
import jax
import jax.numpy as jnp
from jax import lax
from jax.experimental import pallas as pl
from jax.experimental.pallas import tpu as pltpu
from jax.sharding import PartitionSpec as P

BASE = 64
GROUP = 8

def split(v):
    high = v.astype(jnp.bfloat16)
    low = (v - high.astype(jnp.float32)).astype(jnp.bfloat16)
    return high, low

def product(a, b, dims):
    ah, al = split(a)
    bh, bl = split(b)
    f = lambda u, v: lax.dot_general(u, v, (dims, ((), ())), preferred_element_type=jnp.float32)
    return f(ah, bh) + (f(ah, bl) + f(al, bh))

def mm_nt(a, b):
    return product(a, b, ((1,), (1,)))

def mm(a, b):
    return product(a, b, ((1,), (0,)))

def factor_group(scalars):
    n = GROUP
    g = [row[:] for row in scalars]
    unit = [[None] * n for _ in range(n)]
    pivots = []
    inverses = []
    for q in range(n):
        d = g[q][q]
        inv = 1.0 / d
        pivots.append(d)
        inverses.append(inv)
        for i in range(q + 1, n):
            unit[i][q] = g[i][q] * inv
        for i in range(q + 1, n):
            for k in range(q + 1, i + 1):
                g[i][k] = g[i][k] - unit[i][q] * g[k][q]
    w = [[None] * n for _ in range(n)]
    for q in range(n):
        for i in range(q + 1, n):
            acc = unit[i][q]
            for k in range(q + 1, i):
                acc = acc + unit[i][k] * w[k][q]
            w[i][q] = -acc
    return w, pivots, inverses

def base_inverse(s):
    lanes = 2 * BASE
    row = lax.broadcasted_iota(jnp.int32, (BASE, BASE), 0)
    col = lax.broadcasted_iota(jnp.int32, (BASE, BASE), 1)
    eye = jnp.where(row == col, 1.0, 0.0).astype(jnp.float32)
    table = jnp.concatenate([s, eye], axis=1)
    groups = [table[GROUP * h : GROUP * h + GROUP, :] for h in range(BASE // GROUP)]
    shape = (GROUP, lanes)
    sub = lax.broadcasted_iota(jnp.int32, shape, 0)
    spread = lambda v: jnp.broadcast_to(v, shape)
    done = []
    for g in range(BASE // GROUP):
        p = groups[g]
        start = GROUP * g
        cols = [spread(p[:, start + q : start + q + 1]) for q in range(GROUP)]
        scalars = [[spread(cols[q][i : i + 1, :]) if i >= q else None for q in range(GROUP)] for i in range(GROUP)]
        w, pivots, inverses = factor_group(scalars)
        rows = [spread(p[q : q + 1, :]) for q in range(GROUP)]
        reduced = []
        for i in range(GROUP):
            acc = rows[i]
            for q in range(i):
                acc = acc + w[i][q] * rows[q]
            reduced.append(acc)
        for h in range(g + 1, BASE // GROUP):
            t = groups[h]
            cb = [spread(t[:, start + q : start + q + 1]) for q in range(GROUP)]
            for q in range(GROUP):
                v = cb[q]
                for k in range(q):
                    v = v + w[q][k] * cb[k]
                t = t - (v * inverses[q]) * reduced[q]
            groups[h] = t
        out = jnp.zeros(shape, jnp.float32)
        for q in range(GROUP):
            out = jnp.where(sub == q, reduced[q] * lax.rsqrt(pivots[q]), out)
        done.append(out)
    return jnp.concatenate(done, axis=0)[:, BASE:]

def factor_inverse(s_ref, m_ref):
    n = s_ref.shape[0]
    m_ref[...] = jnp.zeros_like(m_ref)

    def solve(at, size):
        if size == BASE:
            m_ref[at : at + size, at : at + size] = base_inverse(s_ref[at : at + size, at : at + size])
            return
        half = size // 2
        lo, mid = slice(at, at + half), slice(at + half, at + size)
        solve(at, half)
        m0 = m_ref[lo, lo]
        below = mm_nt(s_ref[mid, lo], m0)
        s_ref[mid, mid] = s_ref[mid, mid] - mm_nt(below, below)
        w = mm(below, m0)
        solve(at + half, half)
        m_ref[mid, lo] = -mm(m_ref[mid, mid], w)

    solve(0, n)


AXES = ("prow", "pcol")
NB = 256
NEWEST = 63
PLANES = 8
CHUNK = 2 * NB // PLANES
HALF = CHUNK // 2
VMEM = pl.BlockSpec(memory_space=pltpu.VMEM)
SMEM = pl.BlockSpec(memory_space=pltpu.SMEM)
ROW, COLUMN, ROOT, FLIPPED, FIRST, SECOND = range(6)


def chunk_of(info, plane):
    return (plane - info[ROOT] + 1 + PLANES + 4 * info[FLIPPED]) % PLANES


def at_chunk(chunk):
    return pl.ds(pl.multiple_of(chunk * CHUNK, CHUNK), CHUNK)


def chain_kernel(info, own_ref, twin_ref, m_ref, s_ref):
    flip = info[FLIPPED] == 1
    core = info[COLUMN] % 2
    for slot in range(PLANES):
        base = chunk_of(info, (info[ROW] + 1 + slot) % PLANES) * CHUNK
        for ref, side in ((own_ref, core), (twin_ref, 1 - core)):
            v = ref[slot]
            v = jnp.where(flip, jnp.concatenate([v[:, NB:], v[:, :NB]], axis=1), v)
            s_ref[pl.ds(pl.multiple_of(base + side * HALF, HALF), HALF), :] = v
    factor_inverse(s_ref, m_ref)


def chain(info, own, twin):
    return pl.pallas_call(
        chain_kernel,
        out_shape=jax.ShapeDtypeStruct((2 * NB, 2 * NB), jnp.float32),
        in_specs=[SMEM, VMEM, VMEM],
        out_specs=VMEM,
        scratch_shapes=[pltpu.VMEM((2 * NB, 2 * NB), jnp.float32)],
        compiler_params=pltpu.CompilerParams(vmem_limit_bytes=32 * 1024 * 1024),
        name="factor",
    )(info, own, twin)


def dot3(ah, al, bh, bl):
    f = lambda u, v: lax.dot_general(u, v, (((1,), (0,)), ((), ())), preferred_element_type=jnp.float32)
    return f(ah, bh) + (f(ah, bl) + f(al, bh))


def update_kernel(info, m_ref, *refs):
    parts = refs[:PLANES]
    g_ref, a_ref, panels_ref, t_ref, mt_ref, wh, wl, xh, xl = refs[PLANES:]
    step = pl.program_id(0)

    @pl.when(step == 0)
    def _():
        mt_ref[...] = m_ref[...].T
        for slot in range(PLANES):
            rows = slice(slot * CHUNK, (slot + 1) * CHUNK)
            wh[rows], wl[rows] = split(mt_ref[at_chunk(chunk_of(info, (info[ROW] + 1 + slot) % PLANES)), :])
        mh, ml = wh[...].T, wl[...].T
        vh, vl = split(jnp.concatenate([part[HALF:, :] for part in parts], axis=0))
        xh[...], xl[...] = split(dot3(mh, ml, vh, vl))
        for plane in range(PLANES):
            rows = slice(plane * CHUNK, (plane + 1) * CHUNK)
            wh[rows], wl[rows] = split(mt_ref[at_chunk(chunk_of(info, plane)), :])

    columns = g_ref[...].reshape(2 * NB, NB)
    ch, cl = split(columns.T)
    rows = dot3(ch, cl, wh[...], wl[...])
    block = step * PLANES + info[ROW]
    first, second = info[FIRST], info[SECOND]
    panels_ref[0, 0] = rows[:, :NB]
    panels_ref[1, 0] = jnp.where(block != first, rows[:, NB:], 0.0)
    rh, rl = split(rows)
    trail = a_ref[0] - dot3(rh, rl, xh[...], xl[...])
    row_kept = (block != first) & (block != second)
    for t in range(t_ref.shape[2] // NB):
        column = info[COLUMN] + 32 * t
        kept = row_kept & (column != first) & (column != second)
        part = slice(t * NB, (t + 1) * NB)
        t_ref[0, :, part] = jnp.where(kept, trail[:, part], 0.0)


def update(info, inverse, parts, gathered, matrix):
    br, _, width = matrix.shape
    n = 2 * NB
    whole = lambda *shape: pl.BlockSpec(shape, lambda s, info: (0,) * len(shape))
    groups = gathered.shape[0] // PLANES
    return pl.pallas_call(
        update_kernel,
        grid_spec=pltpu.PrefetchScalarGridSpec(
            num_scalar_prefetch=1,
            grid=(br,),
            in_specs=[whole(n, n)]
            + [whole(*part.shape) for part in parts]
            + [
                pl.BlockSpec((PLANES, CHUNK, NB), lambda s, info: (s % groups, 0, s // groups)),
                pl.BlockSpec((1, NB, width), lambda s, info: (s, 0, 0)),
            ],
            out_specs=[
                pl.BlockSpec((2, 1, NB, NB), lambda s, info: (0, s, 0, 0)),
                pl.BlockSpec((1, NB, width), lambda s, info: (s, 0, 0)),
            ],
            scratch_shapes=[pltpu.VMEM((n, n), jnp.float32)] + [pltpu.VMEM((n, n), jnp.bfloat16)] * 2 + [pltpu.VMEM((n, width), jnp.bfloat16)] * 2,
        ),
        out_shape=[
            jax.ShapeDtypeStruct((2, br, NB, NB), jnp.float32),
            jax.ShapeDtypeStruct((br, NB, width), jnp.float32),
        ],
        compiler_params=pltpu.CompilerParams(vmem_limit_bytes=48 * 1024 * 1024),
        name="update",
    )(info, inverse, *parts, gathered, matrix)


def shards(kernel, pivots):
    height, width = lax.axis_size("prow"), lax.axis_size("pcol")
    assert (height, width) == (PLANES, 32)
    br, bc = kernel.shape[0], kernel.shape[3]
    matrix = kernel.reshape(br, NB, bc, NB)
    r = lax.axis_index("prow")
    c = lax.axis_index("pcol")
    flipped = pivots[0] == NEWEST
    other = jnp.where(flipped, pivots[1], pivots[0])
    root_row, root_col, root_t = other % height, other % width, other // width
    info = jnp.stack([r, c, root_row, flipped.astype(jnp.int32), pivots[0], pivots[1]])
    device = lambda row, column: row * width + column
    everyone = [(row, column) for row in range(height) for column in range(width)]
    send = lambda value, to: lax.ppermute(value, AXES, [(device(a, b), device(*to(a, b))) for a, b in everyone])
    up = lambda value, d: send(value, lambda a, b: ((a + d) % height, b))
    core_twin = lambda value: send(value, lambda a, b: (a, b ^ 1))

    def rows_of(block_row, q):
        rows = lax.dynamic_slice(matrix, (block_row, q * CHUNK, 0, 0), (1, CHUNK, bc, NB))
        return rows.reshape(CHUNK, bc * NB)

    block_row = other // height
    own = rows_of(block_row, 1)
    before = up(rows_of(block_row, 0), height - 1)
    after = up(rows_of(block_row, 2), 1)
    second_after = up(rows_of(block_row, 3), 2)
    last = [rows_of(NEWEST // height, (z - root_row - 3) % 4) for z in range(4)]
    newest = jnp.where(r == height - 1, last[(height - 1) % 4], 0.0)
    for z in range(height - 1):
        pairs = [(device(height - 1, k), device(z, k)) for k in range(width)]
        newest = newest + lax.ppermute(last[z % 4], AXES, pairs)
    q = (r - root_row + 1) % height
    piece = jnp.where(q == 0, before, jnp.where(q == 1, own, jnp.where(q == 2, after, jnp.where(q == 3, second_after, newest))))

    moved = send(piece, lambda a, b: (b % height, (b // height) * height + a))
    gathered = lax.all_gather(moved, "pcol", axis=0, tiled=False)

    left = lax.dynamic_slice_in_dim(piece, root_t * NB, NB, 1)
    both = jnp.concatenate([left, piece[:, NB:]], axis=1)
    core, ypos, xpos = c % 2, (c // 2) % 4, c // 8
    rcore, ry, rx = root_col % 2, (root_col // 2) % 4, root_col // 8
    side = lax.broadcasted_iota(jnp.int32, (CHUNK, 2 * NB), 1) < NB
    both = jnp.where(jnp.where(side, core == rcore, core == 1), both, core_twin(both))
    mine = lax.dynamic_slice_in_dim(both, core * HALF, HALF, 0)
    side = side[:HALF]

    def spread(value, position, goal, last, shift):
        source = jnp.where(side, (position - goal) % 4, (position - last) % 4)
        out = value
        for d in range(1, 4):
            out = jnp.where(source == d, send(value, lambda a, b: (a, shift(b, d))), out)
        return out

    mine = spread(mine, xpos, rx, 3, lambda b, d: (b + 8 * d) % 32)
    mine = spread(mine, ypos, ry, 3, lambda b, d: (b // 8) * 8 + (b + 2 * d) % 8)

    mixed = jnp.concatenate([mine, piece], axis=0)
    parts = [up(mixed, d) for d in range(height - 1, 0, -1)] + [mixed]
    ring = jnp.stack([part[:HALF] for part in parts])
    inverse = chain(info, ring, core_twin(ring))
    panels, trailing = update(info, inverse, parts, gathered, matrix.reshape(br, NB, bc * NB))
    return panels.reshape(2, br, 1, NB, NB), trailing.reshape(kernel.shape)


def solution(mesh):
    in_specs = (P(None, "prow", None, None, "pcol", None), P())
    out_specs = (P(None, None, "prow", None, None), P(None, "prow", None, None, "pcol", None))
    return jax.shard_map(shards, mesh=mesh, in_specs=in_specs, out_specs=out_specs, check_vma=False)
```

```python
import jax
import jax.numpy as jnp
from jax import lax
from jax.experimental import pallas as pl
from jax.experimental.pallas import tpu as pltpu
from jax.sharding import PartitionSpec as P

BASE = 64
GROUP = 8


def split(v):
    high = v.astype(jnp.bfloat16)
    low = (v - high.astype(jnp.float32)).astype(jnp.bfloat16)
    return high, low


def dot3(a, b, dims=((1,), (0,))):
    (ah, al), (bh, bl) = a, b
    f = lambda u, v: lax.dot_general(u, v, (dims, ((), ())), preferred_element_type=jnp.float32)
    return f(ah, bh) + (f(ah, bl) + f(al, bh))


def product(a, b, dims=((1,), (0,))):
    return dot3(split(a), split(b), dims)


def factor_group(scalars):
    n = GROUP
    g = [row[:] for row in scalars]
    unit = [[None] * n for _ in range(n)]
    pivots = []
    inverses = []
    for q in range(n):
        d = g[q][q]
        inv = 1.0 / d
        pivots.append(d)
        inverses.append(inv)
        for i in range(q + 1, n):
            unit[i][q] = g[i][q] * inv
        for i in range(q + 1, n):
            for k in range(q + 1, i + 1):
                g[i][k] = g[i][k] - unit[i][q] * g[k][q]
    w = [[None] * n for _ in range(n)]
    for q in range(n):
        for i in range(q + 1, n):
            acc = unit[i][q]
            for k in range(q + 1, i):
                acc = acc + unit[i][k] * w[k][q]
            w[i][q] = -acc
    return w, pivots, inverses


def base_inverse(s):
    lanes = 2 * BASE
    row = lax.broadcasted_iota(jnp.int32, (BASE, BASE), 0)
    col = lax.broadcasted_iota(jnp.int32, (BASE, BASE), 1)
    eye = jnp.where(row == col, 1.0, 0.0).astype(jnp.float32)
    table = jnp.concatenate([s, eye], axis=1)
    groups = [table[GROUP * h : GROUP * h + GROUP, :] for h in range(BASE // GROUP)]
    shape = (GROUP, lanes)
    sub = lax.broadcasted_iota(jnp.int32, shape, 0)
    spread = lambda v: jnp.broadcast_to(v, shape)
    done = []
    for g in range(BASE // GROUP):
        p = groups[g]
        start = GROUP * g
        cols = [spread(p[:, start + q : start + q + 1]) for q in range(GROUP)]
        scalars = [[spread(cols[q][i : i + 1, :]) if i >= q else None for q in range(GROUP)] for i in range(GROUP)]
        w, pivots, inverses = factor_group(scalars)
        rows = [spread(p[q : q + 1, :]) for q in range(GROUP)]
        reduced = []
        for i in range(GROUP):
            acc = rows[i]
            for q in range(i):
                acc = acc + w[i][q] * rows[q]
            reduced.append(acc)
        for h in range(g + 1, BASE // GROUP):
            t = groups[h]
            cb = [spread(t[:, start + q : start + q + 1]) for q in range(GROUP)]
            for q in range(GROUP):
                v = cb[q]
                for k in range(q):
                    v = v + w[q][k] * cb[k]
                t = t - (v * inverses[q]) * reduced[q]
            groups[h] = t
        out = jnp.zeros(shape, jnp.float32)
        for q in range(GROUP):
            out = jnp.where(sub == q, reduced[q] * lax.rsqrt(pivots[q]), out)
        done.append(out)
    return jnp.concatenate(done, axis=0)[:, BASE:]


def pair_inverse(s):
    top = base_inverse(s[:BASE, :BASE])
    below = product(s[BASE:, :BASE], top, ((1,), (1,)))
    rest = s[BASE:, BASE:] - product(below, below, ((1,), (1,)))
    carried = product(below, top)
    bottom = base_inverse(rest)
    corner = -product(bottom, carried)
    return jnp.concatenate(
        [jnp.concatenate([top, jnp.zeros_like(top)], axis=1), jnp.concatenate([corner, bottom], axis=1)], axis=0
    )


def factor_inverse(s_ref, z_ref, m_ref):
    n = s_ref.shape[0]
    size = 2 * BASE
    row = lax.broadcasted_iota(jnp.int32, (n, n), 0)
    col = lax.broadcasted_iota(jnp.int32, (n, n), 1)
    z_ref[...] = jnp.where(row == col, 1.0, 0.0).astype(jnp.float32)

    def step(k, carry):
        here = pl.ds(pl.multiple_of(k * size, size), size)
        inverse = split(pair_inverse(s_ref[here, here]))
        us = split(dot3(inverse, split(s_ref[here, :])))
        uz = dot3(inverse, split(z_ref[here, :]))
        m_ref[here, :] = uz
        uz = split(uz)
        s_ref[...] -= dot3(us, us, ((0,), (0,)))
        z_ref[...] -= dot3(us, uz, ((0,), (0,)))
        return carry

    lax.fori_loop(0, n // size, step, 0)


AXES = ("prow", "pcol")
NB = 256
NEWEST = 63
PLANES = 8
CHUNK = 2 * NB // PLANES
HALF = CHUNK // 2
LANES = 128
VMEM = pl.BlockSpec(memory_space=pltpu.VMEM)
SMEM = pl.BlockSpec(memory_space=pltpu.SMEM)
ROW, COLUMN, ROOT, HELD, FLIPPED, FIRST, SECOND = range(7)
PARAMS = pltpu.CompilerParams(vmem_limit_bytes=48 * 1024 * 1024)


def chunk_of(info, plane):
    return (plane - info[ROOT] + 1 + PLANES) % PLANES


def place_of(info, plane):
    return (chunk_of(info, plane) + PLANES // 2 * info[FLIPPED]) % PLANES


def block_column(ref, t, rows):
    return jnp.concatenate([ref[pl.ds(2 * t + j, rows, stride=4), :] for j in range(2)], axis=1)


def pick_kernel(info, before, own, after, second_after, newest, piece_ref, both_ref):
    q = chunk_of(info, info[ROW])
    for k, ref in enumerate((before, own, after, second_after)):

        @pl.when(q == k)
        def _():
            piece_ref[...] = ref[...]

    @pl.when(q >= PLANES // 2)
    def _():
        piece_ref[...] = newest[...]

    both_ref[:, :NB] = block_column(piece_ref, info[HELD], CHUNK)
    both_ref[:, NB:] = block_column(piece_ref, 1, CHUNK)


def pick(info, *pieces):
    return pl.pallas_call(
        pick_kernel,
        out_shape=[
            jax.ShapeDtypeStruct((4 * CHUNK, LANES), jnp.float32),
            jax.ShapeDtypeStruct((CHUNK, 2 * NB), jnp.float32),
        ],
        in_specs=[SMEM] + [VMEM] * len(pieces),
        out_specs=[VMEM, VMEM],
        compiler_params=PARAMS,
        name="pick",
    )(info, *pieces)


def chain_kernel(info, own_ref, twin_ref, m_ref, s_ref, z_ref):
    flip = info[FLIPPED] == 1
    core = info[COLUMN] % 2
    for slot in range(PLANES):
        base = place_of(info, (info[ROW] + 1 + slot) % PLANES) * CHUNK
        for ref, side in ((own_ref, core), (twin_ref, 1 - core)):
            v = ref[slot]
            v = jnp.where(flip, jnp.concatenate([v[:, NB:], v[:, :NB]], axis=1), v)
            s_ref[pl.ds(pl.multiple_of(base + side * HALF, HALF), HALF), :] = v
    factor_inverse(s_ref, z_ref, m_ref)


def chain(info, own, twin):
    return pl.pallas_call(
        chain_kernel,
        out_shape=jax.ShapeDtypeStruct((2 * NB, 2 * NB), jnp.float32),
        in_specs=[SMEM, VMEM, VMEM],
        out_specs=VMEM,
        scratch_shapes=[pltpu.VMEM((2 * NB, 2 * NB), jnp.float32)] * 2,
        compiler_params=PARAMS,
        name="factor",
    )(info, own, twin)


def update_kernel(info, m_ref, x_ref, g_ref, a_ref, panels_ref, t_ref, mt_ref, wh, wl, xh, xl):
    group, t = pl.program_id(0), pl.program_id(1)
    block = (t * pl.num_programs(0) + group) * PLANES + info[ROW]

    @pl.when((group == 0) & (t == 0))
    def _():
        mt_ref[...] = m_ref[...].T
        for plane in range(PLANES):
            start = pl.multiple_of(place_of(info, plane) * CHUNK, CHUNK)
            rows = slice(plane * CHUNK, (plane + 1) * CHUNK)
            wh[rows], wl[rows] = split(mt_ref[pl.ds(start, CHUNK), :])
        weights = wh[...].T, wl[...].T
        for column in range(2):
            x = jnp.concatenate([block_column(x_ref.at[plane], column, CHUNK) for plane in range(PLANES)], axis=0)
            part = slice(column * NB, (column + 1) * NB)
            xh[:, part], xl[:, part] = split(dot3(weights, split(x)))

    columns = jnp.concatenate([block_column(g_ref.at[plane], t, CHUNK) for plane in range(PLANES)], axis=0)
    rows = dot3(split(columns.T), (wh[...], wl[...]))
    first, second = info[FIRST], info[SECOND]
    panels_ref[0, 0] = rows[:, :NB]
    panels_ref[1, 0] = jnp.where(block != first, rows[:, NB:], 0.0)
    trail = dot3(split(rows), (xh[...], xl[...]))
    row_kept = (block != first) & (block != second)
    for column in range(2):
        number = info[COLUMN] + 32 * column
        kept = row_kept & (number != first) & (number != second)
        for j in range(2):
            where = pl.ds(2 * column + j, NB, stride=4)
            start = column * NB + j * LANES
            t_ref[0, where, :] = jnp.where(kept, a_ref[0, where, :] - trail[:, start : start + LANES], 0.0)


def update(info, inverse, crossing, gathered, flat):
    n = 2 * NB
    br, rows, _ = flat.shape
    groups = gathered.shape[0] // PLANES
    whole = lambda *shape: pl.BlockSpec(shape, lambda k, t, info: (0,) * len(shape))
    block = lambda k, t, info: (t * groups + k, 0, 0)
    return pl.pallas_call(
        update_kernel,
        grid_spec=pltpu.PrefetchScalarGridSpec(
            num_scalar_prefetch=1,
            grid=(groups, br // groups),
            in_specs=[
                whole(n, n),
                whole(*crossing.shape),
                pl.BlockSpec((PLANES, 4 * CHUNK, LANES), lambda k, t, info: (k, 0, 0)),
                pl.BlockSpec((1, rows, LANES), block),
            ],
            out_specs=[
                pl.BlockSpec((2, 1, NB, NB), lambda k, t, info: (0, t * groups + k, 0, 0)),
                pl.BlockSpec((1, rows, LANES), block),
            ],
            scratch_shapes=[pltpu.VMEM((n, n), jnp.float32)] + [pltpu.VMEM((n, n), jnp.bfloat16)] * 4,
        ),
        out_shape=[
            jax.ShapeDtypeStruct((2, br, NB, NB), jnp.float32),
            jax.ShapeDtypeStruct(flat.shape, jnp.float32),
        ],
        compiler_params=PARAMS,
        name="update",
    )(info, inverse, crossing, gathered, flat)


def shards(kernel, pivots):
    height, width = lax.axis_size("prow"), lax.axis_size("pcol")
    assert (height, width) == (PLANES, 32)
    br, bc = kernel.shape[0], kernel.shape[3]
    assert bc == 2
    flat = kernel.reshape(br, NB * bc * NB // LANES, LANES)
    r = lax.axis_index("prow")
    c = lax.axis_index("pcol")
    flipped = pivots[0] == NEWEST
    other = jnp.where(flipped, pivots[1], pivots[0])
    block_row, root_row = other >> 3, other & 7
    root_t, root_col = other >> 5, other & 31
    info = jnp.stack([r, c, root_row, root_t, flipped.astype(jnp.int32), pivots[0], pivots[1]])
    device = lambda row, column: row * width + column
    everyone = [(row, column) for row in range(height) for column in range(width)]
    send = lambda value, to: lax.ppermute(value, AXES, [(device(a, b), device(*to(a, b))) for a, b in everyone])
    up = lambda value, d: send(value, lambda a, b: ((a + d) % height, b))
    core_twin = lambda value: send(value, lambda a, b: (a, b ^ 1))

    piece_rows = 4 * CHUNK
    others = lax.dynamic_slice(flat, (block_row, 0, 0), (1,) + flat.shape[1:])[0]
    part = lambda rows, q: rows[q * piece_rows : (q + 1) * piece_rows]
    before = up(part(others, 0), height - 1)
    after = up(part(others, 2), 1)
    second_after = up(part(others, 3), 2)

    def newest_from(root):
        def run(rows):
            total = jnp.zeros((piece_rows, LANES), jnp.float32)
            for q in range(4):
                plane = (root + 3 + q) % height
                if plane == height - 1:
                    total = jnp.where(r == plane, part(rows, q), total)
                else:
                    pairs = [(device(height - 1, k), device(plane, k)) for k in range(width)]
                    total = total + lax.ppermute(part(rows, q), AXES, pairs)
            return total
        return run

    newest = lax.switch(root_row, [newest_from(root) for root in range(height)], flat[NEWEST // height])
    piece, both = pick(info, before, part(others, 1), after, second_after, newest)

    crossing = lax.all_gather(piece, "prow", axis=0, tiled=False)
    moved = send(piece, lambda a, b: (b % height, (b // height) * height + a))
    gathered = lax.all_gather(moved, "pcol", axis=0, tiled=False)

    core, ypos, xpos = c & 1, (c >> 1) & 3, c >> 3
    rcore, ry, rx = root_col & 1, (root_col >> 1) & 3, root_col >> 3
    side = lax.broadcasted_iota(jnp.int32, (CHUNK, 2 * NB), 1) < NB
    both = jnp.where(jnp.where(side, core == rcore, core == 1), both, core_twin(both))
    mine = lax.dynamic_slice_in_dim(both, core * HALF, HALF, 0)
    side = side[:HALF]

    def spread(value, position, goal, last, shift):
        source = jnp.where(side, (position - goal) & 3, (position - last) & 3)
        out = value
        for d in range(1, 4):
            out = jnp.where(source == d, send(value, lambda a, b: (a, shift(b, d))), out)
        return out

    mine = spread(mine, xpos, rx, 3, lambda b, d: (b + 8 * d) % 32)
    mine = spread(mine, ypos, ry, 3, lambda b, d: (b // 8) * 8 + (b + 2 * d) % 8)
    ring = jnp.stack([up(mine, d) for d in range(height - 1, 0, -1)] + [mine])
    inverse = chain(info, ring, core_twin(ring))
    panels, trailing = update(info, inverse, crossing, gathered, flat)
    return panels.reshape(2, br, 1, NB, NB), trailing.reshape(kernel.shape)


def solution(mesh):
    in_specs = (P(None, "prow", None, None, "pcol", None), P())
    out_specs = (P(None, None, "prow", None, None), P(None, "prow", None, None, "pcol", None))
    return jax.shard_map(shards, mesh=mesh, in_specs=in_specs, out_specs=out_specs, check_vma=False)
```

```python
import jax
import jax.numpy as jnp
from jax import lax
from jax.experimental import pallas as pl
from jax.experimental.pallas import tpu as pltpu
from jax.sharding import PartitionSpec as P

BASE = 64
GROUP = 8


def split(v):
    high = v.astype(jnp.bfloat16)
    low = (v - high.astype(jnp.float32)).astype(jnp.bfloat16)
    return high, low


def dot3(a, b, dims=((1,), (0,))):
    (ah, al), (bh, bl) = a, b
    f = lambda u, v: lax.dot_general(u, v, (dims, ((), ())), preferred_element_type=jnp.float32)
    return f(ah, bh) + (f(ah, bl) + f(al, bh))


def product(a, b, dims=((1,), (0,))):
    return dot3(split(a), split(b), dims)


def factor_group(scalars):
    n = GROUP
    g = [row[:] for row in scalars]
    unit = [[None] * n for _ in range(n)]
    pivots = []
    inverses = []
    for q in range(n):
        d = g[q][q]
        inv = 1.0 / d
        pivots.append(d)
        inverses.append(inv)
        for i in range(q + 1, n):
            unit[i][q] = g[i][q] * inv
        for i in range(q + 1, n):
            for k in range(q + 1, i + 1):
                g[i][k] = g[i][k] - unit[i][q] * g[k][q]
    w = [[None] * n for _ in range(n)]
    for q in range(n):
        for i in range(q + 1, n):
            acc = unit[i][q]
            for k in range(q + 1, i):
                acc = acc + unit[i][k] * w[k][q]
            w[i][q] = -acc
    return w, pivots, inverses


def base_inverse(s):
    lanes = 2 * BASE
    row = lax.broadcasted_iota(jnp.int32, (BASE, BASE), 0)
    col = lax.broadcasted_iota(jnp.int32, (BASE, BASE), 1)
    eye = jnp.where(row == col, 1.0, 0.0).astype(jnp.float32)
    table = jnp.concatenate([s, eye], axis=1)
    groups = [table[GROUP * h : GROUP * h + GROUP, :] for h in range(BASE // GROUP)]
    shape = (GROUP, lanes)
    sub = lax.broadcasted_iota(jnp.int32, shape, 0)
    spread = lambda v: jnp.broadcast_to(v, shape)
    done = []
    for g in range(BASE // GROUP):
        p = groups[g]
        start = GROUP * g
        cols = [spread(p[:, start + q : start + q + 1]) for q in range(GROUP)]
        scalars = [[spread(cols[q][i : i + 1, :]) if i >= q else None for q in range(GROUP)] for i in range(GROUP)]
        w, pivots, inverses = factor_group(scalars)
        rows = [spread(p[q : q + 1, :]) for q in range(GROUP)]
        reduced = []
        for i in range(GROUP):
            acc = rows[i]
            for q in range(i):
                acc = acc + w[i][q] * rows[q]
            reduced.append(acc)
        for h in range(g + 1, BASE // GROUP):
            t = groups[h]
            cb = [spread(t[:, start + q : start + q + 1]) for q in range(GROUP)]
            for q in range(GROUP):
                v = cb[q]
                for k in range(q):
                    v = v + w[q][k] * cb[k]
                t = t - (v * inverses[q]) * reduced[q]
            groups[h] = t
        out = jnp.zeros(shape, jnp.float32)
        for q in range(GROUP):
            out = jnp.where(sub == q, reduced[q] * lax.rsqrt(pivots[q]), out)
        done.append(out)
    return jnp.concatenate(done, axis=0)[:, BASE:]


def pair_inverse(s):
    top = base_inverse(s[:BASE, :BASE])
    below = product(s[BASE:, :BASE], top, ((1,), (1,)))
    rest = s[BASE:, BASE:] - product(below, below, ((1,), (1,)))
    carried = product(below, top)
    bottom = base_inverse(rest)
    corner = -product(bottom, carried)
    return jnp.concatenate(
        [jnp.concatenate([top, jnp.zeros_like(top)], axis=1), jnp.concatenate([corner, bottom], axis=1)], axis=0
    )


def factor_inverse(s_ref, z_ref, m_ref):
    n = s_ref.shape[0]
    size = 2 * BASE
    row = lax.broadcasted_iota(jnp.int32, (n, n), 0)
    col = lax.broadcasted_iota(jnp.int32, (n, n), 1)
    z_ref[...] = jnp.where(row == col, 1.0, 0.0).astype(jnp.float32)

    def step(k, carry):
        here = pl.ds(pl.multiple_of(k * size, size), size)
        inverse = split(pair_inverse(s_ref[here, here]))
        us = split(dot3(inverse, split(s_ref[here, :])))
        uz = dot3(inverse, split(z_ref[here, :]))
        m_ref[here, :] = uz
        uz = split(uz)
        s_ref[...] -= dot3(us, us, ((0,), (0,)))
        z_ref[...] -= dot3(us, uz, ((0,), (0,)))
        return carry

    lax.fori_loop(0, n // size, step, 0)


AXES = ("prow", "pcol")
NB = 256
NEWEST = 63
PLANES = 8
CHUNK = 2 * NB // PLANES
HALF = CHUNK // 2
LANES = 128
VMEM = pl.BlockSpec(memory_space=pltpu.VMEM)
SMEM = pl.BlockSpec(memory_space=pltpu.SMEM)
ROW, COLUMN, ROOT, HELD, FLIPPED, FIRST, SECOND = range(7)
PARAMS = pltpu.CompilerParams(vmem_limit_bytes=48 * 1024 * 1024)


def chunk_of(info, plane):
    return (plane + info[ROOT] // 4 * 4) % PLANES


def place_of(info, plane):
    return (chunk_of(info, plane) + PLANES // 2 * info[FLIPPED]) % PLANES


def block_column(ref, t, rows):
    return jnp.concatenate([ref[pl.ds(2 * t + j, rows, stride=4), :] for j in range(2)], axis=1)


def pick_kernel(info, piece_ref, both_ref):
    both_ref[:, :NB] = block_column(piece_ref, info[HELD], CHUNK)
    both_ref[:, NB:] = block_column(piece_ref, 1, CHUNK)


def pick(info, piece):
    return pl.pallas_call(
        pick_kernel,
        out_shape=jax.ShapeDtypeStruct((CHUNK, 2 * NB), jnp.float32),
        in_specs=[SMEM, VMEM],
        out_specs=VMEM,
        compiler_params=PARAMS,
        name="pick",
    )(info, piece)


def factor_kernel(info, own_ref, twin_ref, x_ref, wh, wl, xh, xl, s_ref, z_ref, m_ref):
    flip = info[FLIPPED] == 1
    core = info[COLUMN] % 2
    for slot in range(PLANES):
        base = place_of(info, (info[ROW] + 1 + slot) % PLANES) * CHUNK
        for ref, side in ((own_ref, core), (twin_ref, 1 - core)):
            v = ref[slot]
            v = jnp.where(flip, jnp.concatenate([v[:, NB:], v[:, :NB]], axis=1), v)
            s_ref[pl.ds(pl.multiple_of(base + side * HALF, HALF), HALF), :] = v
    factor_inverse(s_ref, z_ref, m_ref)
    s_ref[...] = m_ref[...].T
    for plane in range(PLANES):
        start = pl.multiple_of(place_of(info, plane) * CHUNK, CHUNK)
        rows = slice(plane * CHUNK, (plane + 1) * CHUNK)
        wh[rows], wl[rows] = split(s_ref[pl.ds(start, CHUNK), :])
    weights = wh[...].T, wl[...].T
    for column in range(2):
        x = jnp.concatenate([block_column(x_ref.at[plane], column, CHUNK) for plane in range(PLANES)], axis=0)
        part = slice(column * NB, (column + 1) * NB)
        xh[:, part], xl[:, part] = split(dot3(weights, split(x)))


def factor(info, own, twin, crossing):
    n = 2 * NB
    return pl.pallas_call(
        factor_kernel,
        out_shape=[jax.ShapeDtypeStruct((n, n), jnp.bfloat16)] * 4,
        in_specs=[SMEM, VMEM, VMEM, VMEM],
        out_specs=[VMEM] * 4,
        scratch_shapes=[pltpu.VMEM((n, n), jnp.float32)] * 3,
        compiler_params=PARAMS,
        name="factor",
    )(info, own, twin, crossing)


def update_kernel(info, wh, wl, xh, xl, g_ref, a_ref, panels_ref, t_ref):
    group, t = pl.program_id(0), pl.program_id(1)
    block = (t * pl.num_programs(0) + group) * PLANES + info[ROW]
    columns = jnp.concatenate([block_column(g_ref.at[plane], t, CHUNK) for plane in range(PLANES)], axis=0)
    rows = dot3(split(columns.T), (wh[...], wl[...]))
    first, second = info[FIRST], info[SECOND]
    panels_ref[0, 0] = rows[:, :NB]
    panels_ref[1, 0] = jnp.where(block != first, rows[:, NB:], 0.0)
    trail = dot3(split(rows), (xh[...], xl[...]))
    row_kept = (block != first) & (block != second)
    for column in range(2):
        number = info[COLUMN] + 32 * column
        kept = row_kept & (number != first) & (number != second)
        for j in range(2):
            where = pl.ds(2 * column + j, NB, stride=4)
            start = column * NB + j * LANES
            t_ref[0, where, :] = jnp.where(kept, a_ref[0, where, :] - trail[:, start : start + LANES], 0.0)


def update(info, factors, gathered, flat):
    n = 2 * NB
    br, rows, _ = flat.shape
    groups = gathered.shape[0] // PLANES
    block = lambda k, t, info: (t * groups + k, 0, 0)
    return pl.pallas_call(
        update_kernel,
        grid_spec=pltpu.PrefetchScalarGridSpec(
            num_scalar_prefetch=1,
            grid=(groups, br // groups),
            in_specs=[VMEM] * 4
            + [
                pl.BlockSpec((PLANES, 4 * CHUNK, LANES), lambda k, t, info: (k, 0, 0)),
                pl.BlockSpec((1, rows, LANES), block),
            ],
            out_specs=[
                pl.BlockSpec((2, 1, NB, NB), lambda k, t, info: (0, t * groups + k, 0, 0)),
                pl.BlockSpec((1, rows, LANES), block),
            ],
        ),
        out_shape=[
            jax.ShapeDtypeStruct((2, br, NB, NB), jnp.float32),
            jax.ShapeDtypeStruct(flat.shape, jnp.float32),
        ],
        compiler_params=PARAMS,
        name="update",
    )(info, *factors, gathered, flat)


def shards(kernel, pivots):
    height, width = lax.axis_size("prow"), lax.axis_size("pcol")
    assert (height, width) == (PLANES, 32)
    br, bc = kernel.shape[0], kernel.shape[3]
    assert bc == 2
    flat = kernel.reshape(br, NB * bc * NB // LANES, LANES)
    r = lax.axis_index("prow")
    c = lax.axis_index("pcol")
    flipped = pivots[0] == NEWEST
    other = jnp.where(flipped, pivots[1], pivots[0])
    block_row, root_row = other >> 3, other & 7
    root_t, root_col = other >> 5, other & 31
    info = jnp.stack([r, c, root_row, root_t, flipped.astype(jnp.int32), pivots[0], pivots[1]])
    device = lambda row, column: row * width + column
    everyone = [(row, column) for row in range(height) for column in range(width)]
    send = lambda value, to: lax.ppermute(value, AXES, [(device(a, b), device(*to(a, b))) for a, b in everyone])
    up = lambda value, d: send(value, lambda a, b: ((a + d) % height, b))
    core_twin = lambda value: send(value, lambda a, b: (a, b ^ 1))

    piece_rows = 4 * CHUNK
    part = lambda rows, q: rows[q * piece_rows : (q + 1) * piece_rows]

    def scatter_from(root):
        near, quarter = root // 4 * 4, root % 4
        far = 4 - near

        def run(others, newest):
            piece = jnp.zeros((piece_rows, LANES), jnp.float32)
            arrived = []
            for q in range(4):
                if far + q != height - 1:
                    pairs = [(device(height - 1, k), device(far + q, k)) for k in range(width)]
                    arrived.append((far + q, lax.ppermute(part(newest, q), AXES, pairs)))
                if q != quarter:
                    pairs = [(device(half + quarter, k), device(half + q, k)) for half in (0, 4) for k in range(width)]
                    arrived.append((near + q, lax.ppermute(part(others, q), AXES, pairs)))
            arrived.append((root, part(others, quarter)))
            if far == 4:
                arrived.append((height - 1, part(newest, 3)))
            for plane, value in arrived:
                piece = jnp.where(r == plane, value, piece)
            return piece

        return run

    others = lax.dynamic_slice(flat, (block_row, 0, 0), (1,) + flat.shape[1:])[0]
    piece = lax.switch(root_row, [scatter_from(root) for root in range(height)], others, flat[NEWEST // height])
    both = pick(info, piece)

    crossing = lax.all_gather(piece, "prow", axis=0, tiled=False)
    moved = send(piece, lambda a, b: (b % height, (b // height) * height + a))

    core, ypos, xpos = c & 1, (c >> 1) & 3, c >> 3
    rcore, ry, rx = root_col & 1, (root_col >> 1) & 3, root_col >> 3
    side = lax.broadcasted_iota(jnp.int32, (CHUNK, 2 * NB), 1) < NB
    both = jnp.where(jnp.where(side, core == rcore, core == 1), both, core_twin(both))
    mine = lax.dynamic_slice_in_dim(both, core * HALF, HALF, 0)
    side = side[:HALF]

    def spread(value, position, goal, last, shift):
        source = jnp.where(side, (position - goal) & 3, (position - last) & 3)
        out = value
        for d in range(1, 4):
            out = jnp.where(source == d, send(value, lambda a, b: (a, shift(b, d))), out)
        return out

    mine = spread(mine, xpos, rx, 3, lambda b, d: (b + 8 * d) % 32)
    moved, mine = lax.optimization_barrier((moved, mine))
    gathered = lax.all_gather(moved, "pcol", axis=0, tiled=False)
    mine = spread(mine, ypos, ry, 3, lambda b, d: (b // 8) * 8 + (b + 2 * d) % 8)
    ring = jnp.stack([up(mine, d) for d in range(height - 1, 0, -1)] + [mine])
    factors = factor(info, ring, core_twin(ring), crossing)
    panels, trailing = update(info, factors, gathered, flat)
    return panels.reshape(2, br, 1, NB, NB), trailing.reshape(kernel.shape)


def solution(mesh):
    in_specs = (P(None, "prow", None, None, "pcol", None), P())
    out_specs = (P(None, None, "prow", None, None), P(None, "prow", None, None, "pcol", None))
    return jax.shard_map(shards, mesh=mesh, in_specs=in_specs, out_specs=out_specs, check_vma=False)
```

```python
import jax
import jax.numpy as jnp
from jax import lax
from jax.experimental import pallas as pl
from jax.experimental.pallas import tpu as pltpu
from jax.sharding import PartitionSpec as P

BASE = 64
GROUP = 8


def split(v):
    high = v.astype(jnp.bfloat16)
    low = (v - high.astype(jnp.float32)).astype(jnp.bfloat16)
    return high, low


def dot3(a, b, dims=((1,), (0,))):
    (ah, al), (bh, bl) = a, b
    f = lambda u, v: lax.dot_general(u, v, (dims, ((), ())), preferred_element_type=jnp.float32)
    return f(ah, bh) + (f(ah, bl) + f(al, bh))


def stack(b):
    return jnp.concatenate([b[0], b[1], b[0]], axis=0)


def stacked(a, b):
    high, low = split(a)
    return jnp.dot(jnp.concatenate([high, high, low], axis=1), b, preferred_element_type=jnp.float32)


def product(a, b, dims=((1,), (0,))):
    return dot3(split(a), split(b), dims)


def factor_group(scalars):
    n = GROUP
    g = [row[:] for row in scalars]
    unit = [[None] * n for _ in range(n)]
    pivots = []
    inverses = []
    for q in range(n):
        d = g[q][q]
        inv = 1.0 / d
        pivots.append(d)
        inverses.append(inv)
        for i in range(q + 1, n):
            unit[i][q] = g[i][q] * inv
        for i in range(q + 1, n):
            for k in range(q + 1, i + 1):
                g[i][k] = g[i][k] - unit[i][q] * g[k][q]
    w = [[None] * n for _ in range(n)]
    for q in range(n):
        for i in range(q + 1, n):
            acc = unit[i][q]
            for k in range(q + 1, i):
                acc = acc + unit[i][k] * w[k][q]
            w[i][q] = -acc
    return w, pivots, inverses


def base_inverse(s):
    lanes = 2 * BASE
    row = lax.broadcasted_iota(jnp.int32, (BASE, BASE), 0)
    col = lax.broadcasted_iota(jnp.int32, (BASE, BASE), 1)
    eye = jnp.where(row == col, 1.0, 0.0).astype(jnp.float32)
    table = jnp.concatenate([s, eye], axis=1)
    groups = [table[GROUP * h : GROUP * h + GROUP, :] for h in range(BASE // GROUP)]
    shape = (GROUP, lanes)
    sub = lax.broadcasted_iota(jnp.int32, shape, 0)
    spread = lambda v: jnp.broadcast_to(v, shape)
    done = []
    for g in range(BASE // GROUP):
        p = groups[g]
        start = GROUP * g
        cols = [spread(p[:, start + q : start + q + 1]) for q in range(GROUP)]
        scalars = [[spread(cols[q][i : i + 1, :]) if i >= q else None for q in range(GROUP)] for i in range(GROUP)]
        w, pivots, inverses = factor_group(scalars)
        rows = [spread(p[q : q + 1, :]) for q in range(GROUP)]
        reduced = []
        for i in range(GROUP):
            acc = rows[i]
            for q in range(i):
                acc = acc + w[i][q] * rows[q]
            reduced.append(acc)
        for h in range(g + 1, BASE // GROUP):
            t = groups[h]
            cb = [spread(t[:, start + q : start + q + 1]) for q in range(GROUP)]
            for q in range(GROUP):
                v = cb[q]
                for k in range(q):
                    v = v + w[q][k] * cb[k]
                t = t - (v * inverses[q]) * reduced[q]
            groups[h] = t
        out = jnp.zeros(shape, jnp.float32)
        for q in range(GROUP):
            out = jnp.where(sub == q, reduced[q] * lax.rsqrt(pivots[q]), out)
        done.append(out)
    return jnp.concatenate(done, axis=0)[:, BASE:]


def pair_inverse(s):
    top = base_inverse(s[:BASE, :BASE])
    below = product(s[BASE:, :BASE], top, ((1,), (1,)))
    rest = s[BASE:, BASE:] - product(below, below, ((1,), (1,)))
    carried = product(below, top)
    bottom = base_inverse(rest)
    corner = -product(bottom, carried)
    return jnp.concatenate(
        [jnp.concatenate([top, jnp.zeros_like(top)], axis=1), jnp.concatenate([corner, bottom], axis=1)], axis=0
    )


def factor_inverse(s_ref, z_ref, m_ref):
    n = s_ref.shape[0]
    size = 2 * BASE
    row = lax.broadcasted_iota(jnp.int32, (n, n), 0)
    col = lax.broadcasted_iota(jnp.int32, (n, n), 1)
    z_ref[...] = jnp.where(row == col, 1.0, 0.0).astype(jnp.float32)

    def step(k, carry):
        here = pl.ds(pl.multiple_of(k * size, size), size)
        inverse = split(pair_inverse(s_ref[here, here]))
        us = split(dot3(inverse, split(s_ref[here, :])))
        uz = dot3(inverse, split(z_ref[here, :]))
        m_ref[here, :] = uz
        uz = split(uz)
        s_ref[...] -= dot3(us, us, ((0,), (0,)))
        z_ref[...] -= dot3(us, uz, ((0,), (0,)))
        return carry

    lax.fori_loop(0, n // size, step, 0)


AXES = ("prow", "pcol")
NB = 256
NEWEST = 63
PLANES = 8
CHUNK = 2 * NB // PLANES
HALF = CHUNK // 2
LANES = 128
VMEM = pl.BlockSpec(memory_space=pltpu.VMEM)
SMEM = pl.BlockSpec(memory_space=pltpu.SMEM)
ROW, COLUMN, ROOT, HELD, FLIPPED, FIRST, SECOND = range(7)
PARAMS = pltpu.CompilerParams(vmem_limit_bytes=48 * 1024 * 1024)


def chunk_of(info, plane):
    return plane // 2 + PLANES // 2 * ((plane + info[ROOT]) % 2)


def place_of(info, plane):
    return (chunk_of(info, plane) + PLANES // 2 * info[FLIPPED]) % PLANES


def block_column(ref, t, rows):
    return jnp.concatenate([ref[pl.ds(2 * t + j, rows, stride=4), :] for j in range(2)], axis=1)


def pick_kernel(info, piece_ref, both_ref):
    both_ref[:, :NB] = block_column(piece_ref, info[HELD], CHUNK)
    both_ref[:, NB:] = block_column(piece_ref, 1, CHUNK)


def pick(info, piece):
    return pl.pallas_call(
        pick_kernel,
        out_shape=jax.ShapeDtypeStruct((CHUNK, 2 * NB), jnp.float32),
        in_specs=[SMEM, VMEM],
        out_specs=VMEM,
        compiler_params=PARAMS,
        name="pick",
    )(info, piece)


def factor_kernel(info, own_ref, twin_ref, x_ref, w_ref, c_ref, s_ref, z_ref, m_ref):
    flip = info[FLIPPED] == 1
    core = info[COLUMN] % 2
    for slot in range(PLANES):
        base = place_of(info, (info[ROW] + 1 + slot) % PLANES) * CHUNK
        for ref, side in ((own_ref, core), (twin_ref, 1 - core)):
            v = ref[slot]
            v = jnp.where(flip, jnp.concatenate([v[:, NB:], v[:, :NB]], axis=1), v)
            s_ref[pl.ds(pl.multiple_of(base + side * HALF, HALF), HALF), :] = v
    factor_inverse(s_ref, z_ref, m_ref)
    s_ref[...] = m_ref[...].T
    for plane in range(PLANES):
        start = pl.multiple_of(place_of(info, plane) * CHUNK, CHUNK)
        z_ref[plane * CHUNK : (plane + 1) * CHUNK, :] = s_ref[pl.ds(start, CHUNK), :]
    weights = split(z_ref[...])
    w_ref[...] = stack(weights)
    weights = weights[0].T, weights[1].T
    for column in range(2):
        x = jnp.concatenate([block_column(x_ref.at[plane], column, CHUNK) for plane in range(PLANES)], axis=0)
        c_ref[:, column * NB : (column + 1) * NB] = stack(split(dot3(weights, split(x))))


def factor(info, own, twin, crossing):
    n = 2 * NB
    return pl.pallas_call(
        factor_kernel,
        out_shape=[jax.ShapeDtypeStruct((3 * n, n), jnp.bfloat16)] * 2,
        in_specs=[SMEM, VMEM, VMEM, VMEM],
        out_specs=[VMEM] * 2,
        scratch_shapes=[pltpu.VMEM((n, n), jnp.float32)] * 3,
        compiler_params=PARAMS,
        name="factor",
    )(info, own, twin, crossing)


def update_kernel(info, w_ref, c_ref, g_ref, a_ref, panels_ref, t_ref):
    group, t = pl.program_id(0), pl.program_id(1)
    block = (t * pl.num_programs(0) + group) * PLANES + info[ROW]
    columns = jnp.concatenate([block_column(g_ref.at[plane], t, CHUNK) for plane in range(PLANES)], axis=0)
    rows = stacked(columns.T, w_ref[...])
    first, second = info[FIRST], info[SECOND]
    panels_ref[0, 0] = rows[:, :NB]
    panels_ref[1, 0] = jnp.where(block != first, rows[:, NB:], 0.0)
    trail = stacked(rows, c_ref[...])
    row_kept = (block != first) & (block != second)
    for column in range(2):
        number = info[COLUMN] + 32 * column
        kept = row_kept & (number != first) & (number != second)
        for j in range(2):
            where = pl.ds(2 * column + j, NB, stride=4)
            start = column * NB + j * LANES
            t_ref[0, where, :] = jnp.where(kept, a_ref[0, where, :] - trail[:, start : start + LANES], 0.0)


def update(info, factors, gathered, flat):
    br, rows, _ = flat.shape
    groups = gathered.shape[0] // PLANES
    block = lambda k, t, info: (t * groups + k, 0, 0)
    return pl.pallas_call(
        update_kernel,
        grid_spec=pltpu.PrefetchScalarGridSpec(
            num_scalar_prefetch=1,
            grid=(groups, br // groups),
            in_specs=[VMEM] * 2
            + [
                pl.BlockSpec((PLANES, 4 * CHUNK, LANES), lambda k, t, info: (k, 0, 0)),
                pl.BlockSpec((1, rows, LANES), block),
            ],
            out_specs=[
                pl.BlockSpec((2, 1, NB, NB), lambda k, t, info: (0, t * groups + k, 0, 0)),
                pl.BlockSpec((1, rows, LANES), block),
            ],
        ),
        out_shape=[
            jax.ShapeDtypeStruct((2, br, NB, NB), jnp.float32),
            jax.ShapeDtypeStruct(flat.shape, jnp.float32),
        ],
        compiler_params=PARAMS,
        name="update",
    )(info, *factors, gathered, flat)


def shards(kernel, pivots):
    height, width = lax.axis_size("prow"), lax.axis_size("pcol")
    assert (height, width) == (PLANES, 32)
    br, bc = kernel.shape[0], kernel.shape[3]
    assert bc == 2
    flat = kernel.reshape(br, NB * bc * NB // LANES, LANES)
    r = lax.axis_index("prow")
    c = lax.axis_index("pcol")
    flipped = pivots[0] == NEWEST
    other = jnp.where(flipped, pivots[1], pivots[0])
    block_row, root_row = other >> 3, other & 7
    root_t, root_col = other >> 5, other & 31
    info = jnp.stack([r, c, root_row, root_t, flipped.astype(jnp.int32), pivots[0], pivots[1]])
    device = lambda row, column: row * width + column
    everyone = [(row, column) for row in range(height) for column in range(width)]
    send = lambda value, to: lax.ppermute(value, AXES, [(device(a, b), device(*to(a, b))) for a, b in everyone])
    up = lambda value, d: send(value, lambda a, b: ((a + d) % height, b))
    core_twin = lambda value: send(value, lambda a, b: (a, b ^ 1))

    piece_rows = 4 * CHUNK
    part = lambda rows, q: rows[q * piece_rows : (q + 1) * piece_rows]
    line = lambda start, end: [(device(start, k), device(end, k)) for k in range(width)]

    def scatter_from(root):
        parity, quarter = root % 2, root // 2
        away = 1 - parity

        def run(others, newest):
            arrived = []
            for q in range(4):
                plane = 2 * q + away
                if plane != height - 1:
                    arrived.append((plane, lax.ppermute(part(newest, q), AXES, line(height - 1, plane))))
                if q != quarter:
                    plane = 2 * q + parity
                    pairs = line(root, plane)
                    if quarter < 3:
                        pairs = line(2 * quarter, 2 * q) + line(2 * quarter + 1, 2 * q + 1)
                    arrived.append((plane, lax.ppermute(part(others, q), AXES, pairs)))
            arrived.append((root, part(others, quarter)))
            if away == 1:
                arrived.append((height - 1, part(newest, 3)))
            piece = arrived[0][1]
            for plane, value in arrived[1:]:
                piece = jnp.where(r == plane, value, piece)
            return piece

        return run

    others = lax.dynamic_slice(flat, (block_row, 0, 0), (1,) + flat.shape[1:])[0]
    piece = lax.switch(root_row, [scatter_from(root) for root in range(height)], others, flat[NEWEST // height])
    both = pick(info, piece)

    crossing = lax.all_gather(piece, "prow", axis=0, tiled=False)
    moved = send(piece, lambda a, b: (b % height, (b // height) * height + a))

    core, ypos, xpos = c & 1, (c >> 1) & 3, c >> 3
    rcore, ry, rx = root_col & 1, (root_col >> 1) & 3, root_col >> 3
    side = lax.broadcasted_iota(jnp.int32, (CHUNK, 2 * NB), 1) < NB
    both = jnp.where(jnp.where(side, core == rcore, core == 1), both, core_twin(both))
    mine = lax.dynamic_slice_in_dim(both, core * HALF, HALF, 0)
    side = side[:HALF]

    def spread(value, position, goal, last, shift):
        source = jnp.where(side, (position - goal) & 3, (position - last) & 3)
        out = value
        for d in range(1, 4):
            out = jnp.where(source == d, send(value, lambda a, b: (a, shift(b, d))), out)
        return out

    mine = spread(mine, xpos, rx, 3, lambda b, d: (b + 8 * d) % 32)
    moved, mine = lax.optimization_barrier((moved, mine))
    gathered = lax.all_gather(moved, "pcol", axis=0, tiled=False)
    mine = spread(mine, ypos, ry, 3, lambda b, d: (b // 8) * 8 + (b + 2 * d) % 8)
    ring = jnp.stack([up(mine, d) for d in range(height - 1, 0, -1)] + [mine])
    factors = factor(info, ring, core_twin(ring), crossing)
    panels, trailing = update(info, factors, gathered, flat)
    return panels.reshape(2, br, 1, NB, NB), trailing.reshape(kernel.shape)


def solution(mesh):
    in_specs = (P(None, "prow", None, None, "pcol", None), P())
    out_specs = (P(None, None, "prow", None, None), P(None, "prow", None, None, "pcol", None))
    return jax.shard_map(shards, mesh=mesh, in_specs=in_specs, out_specs=out_specs, check_vma=False)
```

```python
import jax
import jax.numpy as jnp
from jax import lax
from jax.experimental import pallas as pl
from jax.experimental.pallas import tpu as pltpu
from jax.sharding import PartitionSpec as P

BASE = 64
GROUP = 8


def split(v):
    high = v.astype(jnp.bfloat16)
    low = (v - high.astype(jnp.float32)).astype(jnp.bfloat16)
    return high, low


def dot3(a, b, dims=((1,), (0,))):
    (ah, al), (bh, bl) = a, b
    f = lambda u, v: lax.dot_general(u, v, (dims, ((), ())), preferred_element_type=jnp.float32)
    return f(ah, bh) + (f(ah, bl) + f(al, bh))


def stack(b):
    return jnp.concatenate([b[0], b[1], b[0]], axis=0)


def stacked(a, b):
    high, low = split(a)
    return jnp.dot(jnp.concatenate([high, high, low], axis=1), b, preferred_element_type=jnp.float32)


def product(a, b, dims=((1,), (0,))):
    return dot3(split(a), split(b), dims)


def factor_group(scalars):
    n = GROUP
    g = [row[:] for row in scalars]
    unit = [[None] * n for _ in range(n)]
    pivots, inverses = [], []
    for q in range(0, n, 2):
        a, b, d = g[q][q], g[q + 1][q], g[q + 1][q + 1]
        det = a * d - b * b
        over = 1.0 / det
        inv = 1.0 / a
        step = b * inv
        below = d - step * b
        pivots += [a, below]
        inverses += [inv, a * over]
        unit[q + 1][q] = step
        for i in range(q + 2, n):
            x, y = g[i][q], g[i][q + 1]
            unit[i][q] = x * inv
            unit[i][q + 1] = (y * a - x * b) * over
        for i in range(q + 2, n):
            x, y = g[i][q], g[i][q + 1]
            u, v = (x * d - y * b) * over, unit[i][q + 1]
            for k in range(q + 2, i + 1):
                g[i][k] = g[i][k] - (u * g[k][q] + v * g[k][q + 1])
    w = [[None] * n for _ in range(n)]
    for q in range(n):
        for i in range(q + 1, n):
            acc = unit[i][q]
            for k in range(q + 1, i):
                acc = acc + unit[i][k] * w[k][q]
            w[i][q] = -acc
    return w, pivots, inverses


def base_inverse(s):
    lanes = 2 * BASE
    row = lax.broadcasted_iota(jnp.int32, (BASE, BASE), 0)
    col = lax.broadcasted_iota(jnp.int32, (BASE, BASE), 1)
    eye = jnp.where(row == col, 1.0, 0.0).astype(jnp.float32)
    table = jnp.concatenate([s, eye], axis=1)
    groups = [table[GROUP * h : GROUP * h + GROUP, :] for h in range(BASE // GROUP)]
    shape = (GROUP, lanes)
    sub = lax.broadcasted_iota(jnp.int32, shape, 0)
    spread = lambda v: jnp.broadcast_to(v, shape)
    done = []
    for g in range(BASE // GROUP):
        p = groups[g]
        start = GROUP * g
        cols = [spread(p[:, start + q : start + q + 1]) for q in range(GROUP)]
        scalars = [[spread(cols[q][i : i + 1, :]) if i >= q else None for q in range(GROUP)] for i in range(GROUP)]
        w, pivots, inverses = factor_group(scalars)
        rows = [spread(p[q : q + 1, :]) for q in range(GROUP)]
        reduced = []
        for i in range(GROUP):
            acc = rows[i]
            for q in range(i):
                acc = acc + w[i][q] * rows[q]
            reduced.append(acc)
        for h in range(g + 1, BASE // GROUP):
            t = groups[h]
            cb = [spread(t[:, start + q : start + q + 1]) for q in range(GROUP)]
            for q in range(GROUP):
                v = cb[q]
                for k in range(q):
                    v = v + w[q][k] * cb[k]
                t = t - (v * inverses[q]) * reduced[q]
            groups[h] = t
        out = jnp.zeros(shape, jnp.float32)
        for q in range(GROUP):
            out = jnp.where(sub == q, reduced[q] * lax.rsqrt(pivots[q]), out)
        done.append(out)
    return jnp.concatenate(done, axis=0)[:, BASE:]


def pair_inverse(s):
    top = base_inverse(s[:BASE, :BASE])
    below = product(s[BASE:, :BASE], top, ((1,), (1,)))
    rest = s[BASE:, BASE:] - product(below, below, ((1,), (1,)))
    carried = product(below, top)
    bottom = base_inverse(rest)
    corner = -product(bottom, carried)
    return jnp.concatenate(
        [jnp.concatenate([top, jnp.zeros_like(top)], axis=1), jnp.concatenate([corner, bottom], axis=1)], axis=0
    )


def factor_inverse(s_ref, z_ref, m_ref):
    n = s_ref.shape[0]
    size = 2 * BASE
    row = lax.broadcasted_iota(jnp.int32, (n, n), 0)
    col = lax.broadcasted_iota(jnp.int32, (n, n), 1)
    z_ref[...] = jnp.where(row == col, 1.0, 0.0).astype(jnp.float32)

    def step(k, carry):
        here = pl.ds(pl.multiple_of(k * size, size), size)
        inverse = split(pair_inverse(s_ref[here, here]))
        us = split(dot3(inverse, split(s_ref[here, :])))
        uz = dot3(inverse, split(z_ref[here, :]))
        m_ref[here, :] = uz
        uz = split(uz)
        s_ref[...] -= dot3(us, us, ((0,), (0,)))
        z_ref[...] -= dot3(us, uz, ((0,), (0,)))
        return carry

    lax.fori_loop(0, n // size, step, 0)


AXES = ("prow", "pcol")
NB = 256
NEWEST = 63
PLANES = 8
CHUNK = 2 * NB // PLANES
HALF = CHUNK // 2
LANES = 128
VMEM = pl.BlockSpec(memory_space=pltpu.VMEM)
SMEM = pl.BlockSpec(memory_space=pltpu.SMEM)
ROW, COLUMN, ROOT, HELD, FLIPPED, FIRST, SECOND = range(7)
MASKS = (0, 4, 2, 6, 1, 5, 3, 7)
PARAMS = pltpu.CompilerParams(vmem_limit_bytes=48 * 1024 * 1024)


def chunk_of(info, plane):
    return plane // 2 + PLANES // 2 * ((plane + info[ROOT]) % 2)


def place_of(info, plane):
    return (chunk_of(info, plane) + PLANES // 2 * info[FLIPPED]) % PLANES


def block_column(ref, t, rows):
    return jnp.concatenate([ref[pl.ds(2 * t + j, rows, stride=4), :] for j in range(2)], axis=1)


def pick_kernel(info, piece_ref, both_ref):
    both_ref[:, :NB] = block_column(piece_ref, info[HELD], CHUNK)
    both_ref[:, NB:] = block_column(piece_ref, 1, CHUNK)


def pick(info, piece):
    return pl.pallas_call(
        pick_kernel,
        out_shape=jax.ShapeDtypeStruct((CHUNK, 2 * NB), jnp.float32),
        in_specs=[SMEM, VMEM],
        out_specs=VMEM,
        compiler_params=PARAMS,
        name="pick",
    )(info, piece)


def factor_kernel(info, own_ref, twin_ref, m_ref, s_ref, z_ref):
    flip = info[FLIPPED] == 1
    core = info[COLUMN] % 2
    for slot in range(PLANES):
        base = place_of(info, info[ROW] ^ MASKS[slot]) * CHUNK
        for ref, side in ((own_ref, core), (twin_ref, 1 - core)):
            v = ref[slot]
            v = jnp.where(flip, jnp.concatenate([v[:, NB:], v[:, :NB]], axis=1), v)
            s_ref[pl.ds(pl.multiple_of(base + side * HALF, HALF), HALF), :] = v
    factor_inverse(s_ref, z_ref, m_ref)


def factor(info, own, twin):
    n = 2 * NB
    return pl.pallas_call(
        factor_kernel,
        out_shape=jax.ShapeDtypeStruct((n, n), jnp.float32),
        in_specs=[SMEM, VMEM, VMEM],
        out_specs=VMEM,
        scratch_shapes=[pltpu.VMEM((n, n), jnp.float32)] * 2,
        compiler_params=PARAMS,
        cost_estimate=pl.CostEstimate(flops=10**9, transcendentals=0, bytes_accessed=9 * 10**7),
        name="factor",
    )(info, own, twin)


def cross_kernel(info, m_ref, near_ref, far_ref, w_ref, c_ref, t_ref, x_ref):
    t_ref[...] = m_ref[...].T
    for plane in range(PLANES):
        start = pl.multiple_of(place_of(info, plane) * CHUNK, CHUNK)
        x_ref[plane * CHUNK : (plane + 1) * CHUNK, :] = t_ref[pl.ds(start, CHUNK), :]
    weights = split(x_ref[...])
    w_ref[...] = stack(weights)
    weights = weights[0].T, weights[1].T
    for slot in range(PLANES):
        ref = (near_ref, far_ref)[slot // 4].at[slot % 4]
        start = pl.multiple_of((info[ROW] ^ MASKS[slot]) * CHUNK, CHUNK)
        for column in range(2):
            x_ref[pl.ds(start, CHUNK), column * NB : (column + 1) * NB] = block_column(ref, column, CHUNK)
    c_ref[...] = stack(split(dot3(weights, split(x_ref[...]))))


def cross(info, inverse, near, far):
    n = 2 * NB
    return pl.pallas_call(
        cross_kernel,
        out_shape=[jax.ShapeDtypeStruct((3 * n, n), jnp.bfloat16)] * 2,
        in_specs=[SMEM] + [VMEM] * 3,
        out_specs=[VMEM] * 2,
        scratch_shapes=[pltpu.VMEM((n, n), jnp.float32)] * 2,
        compiler_params=PARAMS,
        name="cross",
    )(info, inverse, near, far)


def update_kernel(info, w_ref, c_ref, g_ref, a_ref, panels_ref, t_ref):
    group, t = pl.program_id(0), pl.program_id(1)
    block = (t * pl.num_programs(0) + group) * PLANES + info[ROW]
    columns = jnp.concatenate([block_column(g_ref.at[plane], t, CHUNK) for plane in range(PLANES)], axis=0)
    rows = stacked(columns.T, w_ref[...])
    first, second = info[FIRST], info[SECOND]
    panels_ref[0, 0] = rows[:, :NB]
    panels_ref[1, 0] = jnp.where(block != first, rows[:, NB:], 0.0)
    trail = stacked(rows, c_ref[...])
    row_kept = (block != first) & (block != second)
    for column in range(2):
        number = info[COLUMN] + 32 * column
        kept = row_kept & (number != first) & (number != second)
        for j in range(2):
            where = pl.ds(2 * column + j, NB, stride=4)
            start = column * NB + j * LANES
            t_ref[0, where, :] = jnp.where(kept, a_ref[0, where, :] - trail[:, start : start + LANES], 0.0)


def update(info, factors, gathered, flat):
    br, rows, _ = flat.shape
    groups = gathered.shape[0] // PLANES
    block = lambda k, t, info: (t * groups + k, 0, 0)
    return pl.pallas_call(
        update_kernel,
        grid_spec=pltpu.PrefetchScalarGridSpec(
            num_scalar_prefetch=1,
            grid=(groups, br // groups),
            in_specs=[VMEM] * 2
            + [
                pl.BlockSpec((PLANES, 4 * CHUNK, LANES), lambda k, t, info: (k, 0, 0)),
                pl.BlockSpec((1, rows, LANES), block),
            ],
            out_specs=[
                pl.BlockSpec((2, 1, NB, NB), lambda k, t, info: (0, t * groups + k, 0, 0)),
                pl.BlockSpec((1, rows, LANES), block),
            ],
        ),
        out_shape=[
            jax.ShapeDtypeStruct((2, br, NB, NB), jnp.float32),
            jax.ShapeDtypeStruct(flat.shape, jnp.float32),
        ],
        compiler_params=PARAMS,
        name="update",
    )(info, *factors, gathered, flat)


def shards(kernel, pivots):
    height, width = lax.axis_size("prow"), lax.axis_size("pcol")
    assert (height, width) == (PLANES, 32)
    br, bc = kernel.shape[0], kernel.shape[3]
    assert bc == 2
    flat = kernel.reshape(br, NB * bc * NB // LANES, LANES)
    r = lax.axis_index("prow")
    c = lax.axis_index("pcol")
    flipped = pivots[0] == NEWEST
    other = jnp.where(flipped, pivots[1], pivots[0])
    block_row, root_row = other >> 3, other & 7
    root_t, root_col = other >> 5, other & 31
    info = jnp.stack([r, c, root_row, root_t, flipped.astype(jnp.int32), pivots[0], pivots[1]])
    device = lambda row, column: row * width + column
    everyone = [(row, column) for row in range(height) for column in range(width)]
    send = lambda value, to: lax.ppermute(value, AXES, [(device(a, b), device(*to(a, b))) for a, b in everyone])
    double = lambda value, mask: jnp.concatenate([value, send(value, lambda a, b: (a ^ mask, b))], axis=0)
    tie = lambda *values: lax.optimization_barrier(values)
    core_twin = lambda value: send(value, lambda a, b: (a, b ^ 1))

    piece_rows = 4 * CHUNK
    part = lambda rows, q: rows[q * piece_rows : (q + 1) * piece_rows]
    line = lambda start, end: [(device(start, k), device(end, k)) for k in range(width)]

    def scatter_from(root):
        parity, quarter = root % 2, root // 2
        away = 1 - parity

        def run(others, newest):
            arrived = []
            for q in range(4):
                plane = 2 * q + away
                if plane != height - 1:
                    arrived.append((plane, lax.ppermute(part(newest, q), AXES, line(height - 1, plane))))
                if q != quarter:
                    plane = 2 * q + parity
                    pairs = line(root, plane)
                    if quarter < 3:
                        pairs = line(2 * quarter, 2 * q) + line(2 * quarter + 1, 2 * q + 1)
                    arrived.append((plane, lax.ppermute(part(others, q), AXES, pairs)))
            arrived.append((root, part(others, quarter)))
            if away == 1:
                arrived.append((height - 1, part(newest, 3)))
            piece = arrived[0][1]
            for plane, value in arrived[1:]:
                piece = jnp.where(r == plane, value, piece)
            return piece

        return run

    others = lax.dynamic_slice(flat, (block_row, 0, 0), (1,) + flat.shape[1:])[0]
    rows = tie(others, flat[NEWEST // height])
    piece = lax.switch(root_row, [scatter_from(root) for root in range(height)], *rows)
    both = pick(info, piece)

    moved = send(piece, lambda a, b: (b % height, (b // height) * height + a))

    crossing = double(piece[None], 4)

    core, ypos, xpos = c & 1, (c >> 1) & 3, c >> 3
    rcore, ry, rx = root_col & 1, (root_col >> 1) & 3, root_col >> 3
    side = lax.broadcasted_iota(jnp.int32, (CHUNK, 2 * NB), 1) < NB
    both = jnp.where(jnp.where(side, core == rcore, core == 1), both, core_twin(both))
    mine = lax.dynamic_slice_in_dim(both, core * HALF, HALF, 0)
    side = side[:HALF]

    def spread(value, position, goal, last, shift):
        source = jnp.where(side, (position - goal) & 3, (position - last) & 3)
        out = value
        for d in range(1, 4):
            out = jnp.where(source == d, send(value, lambda a, b: (a, shift(b, d))), out)
        return out

    mine = spread(mine, xpos, rx, 3, lambda b, d: (b + 8 * d) % 32)
    moved, crossing, mine = tie(moved, crossing, mine)
    gathered = lax.all_gather(moved, "pcol", axis=0, tiled=False)
    crossing = double(crossing, 2)
    mine = spread(mine, ypos, ry, 3, lambda b, d: (b // 8) * 8 + (b + 2 * d) % 8)
    crossing, mine = tie(crossing, mine)
    beyond = send(crossing, lambda a, b: (a ^ 1, b))
    ring = double(double(double(mine[None], 4), 2), 1)
    factors = cross(info, factor(info, ring, core_twin(ring)), crossing, beyond)
    panels, trailing = update(info, factors, gathered, flat)
    return panels.reshape(2, br, 1, NB, NB), trailing.reshape(kernel.shape)


def solution(mesh):
    in_specs = (P(None, "prow", None, None, "pcol", None), P())
    out_specs = (P(None, None, "prow", None, None), P(None, "prow", None, None, "pcol", None))
    return jax.shard_map(shards, mesh=mesh, in_specs=in_specs, out_specs=out_specs, check_vma=False)
```

```python
import jax
import jax.numpy as jnp
from jax import lax
from jax.experimental import pallas as pl
from jax.experimental.pallas import tpu as pltpu
from jax.sharding import PartitionSpec as P

BASE = 64
GROUP = 8


def split(v):
    high = v.astype(jnp.bfloat16)
    low = (v - high.astype(jnp.float32)).astype(jnp.bfloat16)
    return high, low


def dot3(a, b, dims=((1,), (0,))):
    (ah, al), (bh, bl) = a, b
    f = lambda u, v: lax.dot_general(u, v, (dims, ((), ())), preferred_element_type=jnp.float32)
    return f(ah, bh) + (f(ah, bl) + f(al, bh))


def stack(b):
    return jnp.concatenate([b[0], b[1], b[0]], axis=0)


def stacked(a, b):
    high, low = split(a)
    return jnp.dot(jnp.concatenate([high, high, low], axis=1), b, preferred_element_type=jnp.float32)


def product(a, b, dims=((1,), (0,))):
    return dot3(split(a), split(b), dims)


def factor_group(scalars):
    n = GROUP
    g = [row[:] for row in scalars]
    unit = [[None] * n for _ in range(n)]
    pivots, inverses = [], []
    for q in range(0, n, 2):
        a, b, d = g[q][q], g[q + 1][q], g[q + 1][q + 1]
        det = a * d - b * b
        over = 1.0 / det
        inv = 1.0 / a
        step = b * inv
        below = d - step * b
        pivots += [a, below]
        inverses += [inv, a * over]
        unit[q + 1][q] = step
        for i in range(q + 2, n):
            x, y = g[i][q], g[i][q + 1]
            unit[i][q] = x * inv
            unit[i][q + 1] = (y * a - x * b) * over
        for i in range(q + 2, n):
            x, y = g[i][q], g[i][q + 1]
            u, v = (x * d - y * b) * over, unit[i][q + 1]
            for k in range(q + 2, i + 1):
                g[i][k] = g[i][k] - (u * g[k][q] + v * g[k][q + 1])
    w = [[None] * n for _ in range(n)]
    for q in range(n):
        for i in range(q + 1, n):
            acc = unit[i][q]
            for k in range(q + 1, i):
                acc = acc + unit[i][k] * w[k][q]
            w[i][q] = -acc
    return w, pivots, inverses


def base_inverse(s):
    lanes = 2 * BASE
    row = lax.broadcasted_iota(jnp.int32, (BASE, BASE), 0)
    col = lax.broadcasted_iota(jnp.int32, (BASE, BASE), 1)
    eye = jnp.where(row == col, 1.0, 0.0).astype(jnp.float32)
    table = jnp.concatenate([s, eye], axis=1)
    groups = [table[GROUP * h : GROUP * h + GROUP, :] for h in range(BASE // GROUP)]
    shape = (GROUP, lanes)
    sub = lax.broadcasted_iota(jnp.int32, shape, 0)
    spread = lambda v: jnp.broadcast_to(v, shape)
    done = []
    for g in range(BASE // GROUP):
        p = groups[g]
        start = GROUP * g
        cols = [spread(p[:, start + q : start + q + 1]) for q in range(GROUP)]
        scalars = [[spread(cols[q][i : i + 1, :]) if i >= q else None for q in range(GROUP)] for i in range(GROUP)]
        w, pivots, inverses = factor_group(scalars)
        rows = [spread(p[q : q + 1, :]) for q in range(GROUP)]
        reduced = []
        for i in range(GROUP):
            acc = rows[i]
            for q in range(i):
                acc = acc + w[i][q] * rows[q]
            reduced.append(acc)
        for h in range(g + 1, BASE // GROUP):
            t = groups[h]
            cb = [spread(t[:, start + q : start + q + 1]) for q in range(GROUP)]
            for q in range(GROUP):
                v = cb[q]
                for k in range(q):
                    v = v + w[q][k] * cb[k]
                t = t - (v * inverses[q]) * reduced[q]
            groups[h] = t
        out = jnp.zeros(shape, jnp.float32)
        for q in range(GROUP):
            out = jnp.where(sub == q, reduced[q] * lax.rsqrt(pivots[q]), out)
        done.append(out)
    return jnp.concatenate(done, axis=0)[:, BASE:]


def pair_inverse(s):
    top = base_inverse(s[:BASE, :BASE])
    below = product(s[BASE:, :BASE], top, ((1,), (1,)))
    rest = s[BASE:, BASE:] - product(below, below, ((1,), (1,)))
    carried = product(below, top)
    bottom = base_inverse(rest)
    corner = -product(bottom, carried)
    return jnp.concatenate(
        [jnp.concatenate([top, jnp.zeros_like(top)], axis=1), jnp.concatenate([corner, bottom], axis=1)], axis=0
    )


def factor_inverse(s_ref, z_ref, m_ref):
    n = s_ref.shape[0]
    size = 2 * BASE
    row = lax.broadcasted_iota(jnp.int32, (n, n), 0)
    col = lax.broadcasted_iota(jnp.int32, (n, n), 1)
    z_ref[...] = jnp.where(row == col, 1.0, 0.0).astype(jnp.float32)

    def step(k, carry):
        here = pl.ds(pl.multiple_of(k * size, size), size)
        inverse = split(pair_inverse(s_ref[here, here]))
        us = split(dot3(inverse, split(s_ref[here, :])))
        uz = dot3(inverse, split(z_ref[here, :]))
        m_ref[here, :] = uz
        uz = split(uz)
        s_ref[...] -= dot3(us, us, ((0,), (0,)))
        z_ref[...] -= dot3(us, uz, ((0,), (0,)))
        return carry

    lax.fori_loop(0, n // size, step, 0)


AXES = ("prow", "pcol")
NB = 256
NEWEST = 63
PLANES = 8
CHUNK = 2 * NB // PLANES
HALF = CHUNK // 2
LANES = 128
VMEM = pl.BlockSpec(memory_space=pltpu.VMEM)
SMEM = pl.BlockSpec(memory_space=pltpu.SMEM)
ROW, COLUMN, ROOT, HELD, FLIPPED, FIRST, SECOND = range(7)
MASKS = (0, 4, 2, 6, 1, 5, 3, 7)
PARAMS = pltpu.CompilerParams(vmem_limit_bytes=48 * 1024 * 1024)


def chunk_of(info, plane):
    return plane // 2 + PLANES // 2 * ((plane + info[ROOT]) % 2)


def place_of(info, plane):
    return (chunk_of(info, plane) + PLANES // 2 * info[FLIPPED]) % PLANES


def block_column(ref, t, rows):
    return jnp.concatenate([ref[pl.ds(2 * t + j, rows, stride=4), :] for j in range(2)], axis=1)


def pick_kernel(info, piece_ref, both_ref):
    both_ref[:, :NB] = block_column(piece_ref, info[HELD], CHUNK)
    both_ref[:, NB:] = block_column(piece_ref, 1, CHUNK)


def pick(info, piece):
    return pl.pallas_call(
        pick_kernel,
        out_shape=jax.ShapeDtypeStruct((CHUNK, 2 * NB), jnp.float32),
        in_specs=[SMEM, VMEM],
        out_specs=VMEM,
        compiler_params=PARAMS,
        name="pick",
    )(info, piece)


def factor_kernel(info, own_ref, twin_ref, m_ref, s_ref, z_ref):
    flip = info[FLIPPED] == 1
    core = info[COLUMN] % 2
    for slot in range(PLANES):
        base = place_of(info, info[ROW] ^ MASKS[slot]) * CHUNK
        for ref, side in ((own_ref, core), (twin_ref, 1 - core)):
            v = ref[slot]
            v = jnp.where(flip, jnp.concatenate([v[:, NB:], v[:, :NB]], axis=1), v)
            s_ref[pl.ds(pl.multiple_of(base + side * HALF, HALF), HALF), :] = v
    factor_inverse(s_ref, z_ref, m_ref)


def factor(info, own, twin):
    n = 2 * NB
    return pl.pallas_call(
        factor_kernel,
        out_shape=jax.ShapeDtypeStruct((n, n), jnp.float32),
        in_specs=[SMEM, VMEM, VMEM],
        out_specs=VMEM,
        scratch_shapes=[pltpu.VMEM((n, n), jnp.float32)] * 2,
        compiler_params=PARAMS,
        cost_estimate=pl.CostEstimate(flops=10**9, transcendentals=0, bytes_accessed=9 * 10**7),
        name="factor",
    )(info, own, twin)


def cross_kernel(info, m_ref, near_ref, far_ref, w_ref, c_ref, t_ref, x_ref):
    t_ref[...] = m_ref[...].T
    for plane in range(PLANES):
        start = pl.multiple_of(place_of(info, plane) * CHUNK, CHUNK)
        x_ref[plane * CHUNK : (plane + 1) * CHUNK, :] = t_ref[pl.ds(start, CHUNK), :]
    weights = split(x_ref[...])
    w_ref[...] = stack(weights)
    weights = weights[0].T, weights[1].T
    for slot in range(PLANES):
        ref = (near_ref, far_ref)[slot // 4].at[slot % 4]
        start = pl.multiple_of((info[ROW] ^ MASKS[slot]) * CHUNK, CHUNK)
        for column in range(2):
            x_ref[pl.ds(start, CHUNK), column * NB : (column + 1) * NB] = block_column(ref, column, CHUNK)
    c_ref[...] = stack(split(dot3(weights, split(x_ref[...]))))


def cross(info, inverse, near, far):
    n = 2 * NB
    return pl.pallas_call(
        cross_kernel,
        out_shape=[jax.ShapeDtypeStruct((3 * n, n), jnp.bfloat16)] * 2,
        in_specs=[SMEM] + [VMEM] * 3,
        out_specs=[VMEM] * 2,
        scratch_shapes=[pltpu.VMEM((n, n), jnp.float32)] * 2,
        compiler_params=PARAMS,
        name="cross",
    )(info, inverse, near, far)


def update_kernel(info, w_ref, c_ref, g_ref, a_ref, panels_ref, t_ref):
    group = pl.program_id(0)
    first, second = info[FIRST], info[SECOND]
    for t in range(2):
        block = (t * pl.num_programs(0) + group) * PLANES + info[ROW]
        columns = jnp.concatenate([block_column(g_ref.at[plane], t, CHUNK) for plane in range(PLANES)], axis=0)
        rows = stacked(columns.T, w_ref[...])
        row_kept = (block != first) & (block != second)
        panels_ref[0, t, 0] = rows[:, :NB]
        panels_ref[1, t, 0] = jnp.where(block != first, rows[:, NB:], 0.0)
        trail = stacked(rows, c_ref[...])
        for column in range(2):
            number = info[COLUMN] + 32 * column
            kept = row_kept & (number != first) & (number != second)
            for j in range(2):
                where = pl.ds(2 * column + j, NB, stride=4)
                start = column * NB + j * LANES
                t_ref[t, 0, where, :] = jnp.where(kept, a_ref[t, 0, where, :] - trail[:, start : start + LANES], 0.0)


def update(info, factors, gathered, flat):
    br, rows, _ = flat.shape
    groups = gathered.shape[0] // PLANES
    block = lambda k, info: (0, k, 0, 0)
    return pl.pallas_call(
        update_kernel,
        grid_spec=pltpu.PrefetchScalarGridSpec(
            num_scalar_prefetch=1,
            grid=(groups,),
            in_specs=[VMEM] * 2
            + [
                pl.BlockSpec((PLANES, 4 * CHUNK, LANES), lambda k, info: (k, 0, 0)),
                pl.BlockSpec((2, 1, rows, LANES), block),
            ],
            out_specs=[
                pl.BlockSpec((2, 2, 1, NB, NB), lambda k, info: (0, 0, k, 0, 0)),
                pl.BlockSpec((2, 1, rows, LANES), block),
            ],
        ),
        out_shape=[
            jax.ShapeDtypeStruct((2, 2, groups, NB, NB), jnp.float32),
            jax.ShapeDtypeStruct((2, groups) + flat.shape[1:], jnp.float32),
        ],
        compiler_params=PARAMS,
        name="update",
    )(info, *factors, gathered, flat.reshape((2, groups) + flat.shape[1:]))


def shards(kernel, pivots):
    height, width = lax.axis_size("prow"), lax.axis_size("pcol")
    assert (height, width) == (PLANES, 32)
    br, bc = kernel.shape[0], kernel.shape[3]
    assert bc == 2
    flat = kernel.reshape(br, NB * bc * NB // LANES, LANES)
    r = lax.axis_index("prow")
    c = lax.axis_index("pcol")
    flipped = pivots[0] == NEWEST
    other = jnp.where(flipped, pivots[1], pivots[0])
    block_row, root_row = other >> 3, other & 7
    root_t, root_col = other >> 5, other & 31
    info = jnp.stack([r, c, root_row, root_t, flipped.astype(jnp.int32), pivots[0], pivots[1]])
    device = lambda row, column: row * width + column
    everyone = [(row, column) for row in range(height) for column in range(width)]
    send = lambda value, to: lax.ppermute(value, AXES, [(device(a, b), device(*to(a, b))) for a, b in everyone])
    double = lambda value, mask: jnp.concatenate([value, send(value, lambda a, b: (a ^ mask, b))], axis=0)
    tie = lambda *values: lax.optimization_barrier(values)
    core_twin = lambda value: send(value, lambda a, b: (a, b ^ 1))

    piece_rows = 4 * CHUNK
    part = lambda rows, q: rows[q * piece_rows : (q + 1) * piece_rows]
    line = lambda start, end: [(device(start, k), device(end, k)) for k in range(width)]

    def scatter_from(root):
        parity, quarter = root % 2, root // 2
        away = 1 - parity

        def run(others, newest):
            arrived = []
            for q in range(4):
                plane = 2 * q + away
                if plane != height - 1:
                    arrived.append((plane, lax.ppermute(part(newest, q), AXES, line(height - 1, plane))))
                if q != quarter:
                    plane = 2 * q + parity
                    pairs = line(root, plane)
                    if quarter in (1, 2):
                        pairs = line(2 * quarter, 2 * q) + line(2 * quarter + 1, 2 * q + 1)
                    arrived.append((plane, lax.ppermute(part(others, q), AXES, pairs)))
            arrived.append((root, part(others, quarter)))
            if away == 1:
                arrived.append((height - 1, part(newest, 3)))
            piece = arrived[0][1]
            for plane, value in arrived[1:]:
                piece = jnp.where(r == plane, value, piece)
            return piece

        return run

    others = lax.dynamic_slice(flat, (block_row, 0, 0), (1,) + flat.shape[1:])[0]
    rows = tie(others, flat[NEWEST // height])
    piece = lax.switch(root_row, [scatter_from(root) for root in range(height)], *rows)
    both = pick(info, piece)

    moved = send(piece, lambda a, b: (b % height, (b // height) * height + a))

    crossing = double(piece[None], 4)

    core, ypos, xpos = c & 1, (c >> 1) & 3, c >> 3
    rcore, ry, rx = root_col & 1, (root_col >> 1) & 3, root_col >> 3
    side = lax.broadcasted_iota(jnp.int32, (CHUNK, 2 * NB), 1) < NB
    both = jnp.where(jnp.where(side, core == rcore, core == 1), both, core_twin(both))
    mine = lax.dynamic_slice_in_dim(both, core * HALF, HALF, 0)
    side = side[:HALF]

    def spread(value, position, goal, last, shift):
        source = jnp.where(side, (position - goal) & 3, (position - last) & 3)
        out = value
        for d in range(1, 4):
            out = jnp.where(source == d, send(value, lambda a, b: (a, shift(b, d))), out)
        return out

    mine = spread(mine, xpos, rx, 3, lambda b, d: (b + 8 * d) % 32)
    moved, crossing, mine = tie(moved, crossing, mine)
    gathered = lax.all_gather(moved, "pcol", axis=0, tiled=False)
    crossing = double(crossing, 2)
    mine = spread(mine, ypos, ry, 3, lambda b, d: (b // 8) * 8 + (b + 2 * d) % 8)
    ring = double(double(mine[None], 4), 2)
    crossing, ring = tie(crossing, ring)
    beyond = send(crossing, lambda a, b: (a ^ 1, b))
    ring = double(ring, 1)
    factors = cross(info, factor(info, ring, core_twin(ring)), crossing, beyond)
    panels, trailing = update(info, factors, gathered, flat)
    return panels.reshape(2, br, 1, NB, NB), trailing.reshape(kernel.shape)


def solution(mesh):
    in_specs = (P(None, "prow", None, None, "pcol", None), P())
    out_specs = (P(None, None, "prow", None, None), P(None, "prow", None, None, "pcol", None))
    return jax.shard_map(shards, mesh=mesh, in_specs=in_specs, out_specs=out_specs, check_vma=False)
```

```python
import jax
import jax.numpy as jnp
from jax import lax
from jax.experimental import pallas as pl
from jax.experimental.pallas import tpu as pltpu
from jax.sharding import PartitionSpec as P

BASE = 64
GROUP = 8


def split(v):
    high = v.astype(jnp.bfloat16)
    low = (v - high.astype(jnp.float32)).astype(jnp.bfloat16)
    return high, low


def dot3(a, b, dims=((1,), (0,))):
    (ah, al), (bh, bl) = a, b
    f = lambda u, v: lax.dot_general(u, v, (dims, ((), ())), preferred_element_type=jnp.float32)
    return f(ah, bh) + (f(ah, bl) + f(al, bh))


def stack(b):
    return jnp.concatenate([b[0], b[1], b[0]], axis=0)


def stacked(a, b):
    high, low = split(a)
    return jnp.dot(jnp.concatenate([high, high, low], axis=1), b, preferred_element_type=jnp.float32)


def product(a, b, dims=((1,), (0,))):
    return dot3(split(a), split(b), dims)


def factor_group(scalars):
    n = GROUP
    g = [row[:] for row in scalars]
    unit = [[None] * n for _ in range(n)]
    pivots, inverses = [], []
    for q in range(0, n, 2):
        a, b, d = g[q][q], g[q + 1][q], g[q + 1][q + 1]
        det = a * d - b * b
        over = 1.0 / det
        inv = 1.0 / a
        step = b * inv
        below = d - step * b
        pivots += [a, below]
        inverses += [inv, a * over]
        unit[q + 1][q] = step
        for i in range(q + 2, n):
            x, y = g[i][q], g[i][q + 1]
            unit[i][q] = x * inv
            unit[i][q + 1] = (y * a - x * b) * over
        for i in range(q + 2, n):
            x, y = g[i][q], g[i][q + 1]
            u, v = (x * d - y * b) * over, unit[i][q + 1]
            for k in range(q + 2, i + 1):
                g[i][k] = g[i][k] - (u * g[k][q] + v * g[k][q + 1])
    w = [[None] * n for _ in range(n)]
    for q in range(n):
        for i in range(q + 1, n):
            acc = unit[i][q]
            for k in range(q + 1, i):
                acc = acc + unit[i][k] * w[k][q]
            w[i][q] = -acc
    return w, pivots, inverses


def base_inverse(s):
    lanes = 2 * BASE
    row = lax.broadcasted_iota(jnp.int32, (BASE, BASE), 0)
    col = lax.broadcasted_iota(jnp.int32, (BASE, BASE), 1)
    eye = jnp.where(row == col, 1.0, 0.0).astype(jnp.float32)
    table = jnp.concatenate([s, eye], axis=1)
    groups = [table[GROUP * h : GROUP * h + GROUP, :] for h in range(BASE // GROUP)]
    shape = (GROUP, lanes)
    sub = lax.broadcasted_iota(jnp.int32, shape, 0)
    spread = lambda v: jnp.broadcast_to(v, shape)
    done = []
    for g in range(BASE // GROUP):
        p = groups[g]
        start = GROUP * g
        cols = [spread(p[:, start + q : start + q + 1]) for q in range(GROUP)]
        scalars = [[spread(cols[q][i : i + 1, :]) if i >= q else None for q in range(GROUP)] for i in range(GROUP)]
        w, pivots, inverses = factor_group(scalars)
        rows = [spread(p[q : q + 1, :]) for q in range(GROUP)]
        reduced = []
        for i in range(GROUP):
            acc = rows[i]
            for q in range(i):
                acc = acc + w[i][q] * rows[q]
            reduced.append(acc)
        for h in range(g + 1, BASE // GROUP):
            t = groups[h]
            cb = [spread(t[:, start + q : start + q + 1]) for q in range(GROUP)]
            for q in range(GROUP):
                v = cb[q]
                for k in range(q):
                    v = v + w[q][k] * cb[k]
                t = t - (v * inverses[q]) * reduced[q]
            groups[h] = t
        out = jnp.zeros(shape, jnp.float32)
        for q in range(GROUP):
            out = jnp.where(sub == q, reduced[q] * lax.rsqrt(pivots[q]), out)
        done.append(out)
    return jnp.concatenate(done, axis=0)[:, BASE:]


def pair_inverse(s):
    top = base_inverse(s[:BASE, :BASE])
    below = product(s[BASE:, :BASE], top, ((1,), (1,)))
    rest = s[BASE:, BASE:] - product(below, below, ((1,), (1,)))
    carried = product(below, top)
    bottom = base_inverse(rest)
    corner = -product(bottom, carried)
    return jnp.concatenate(
        [jnp.concatenate([top, jnp.zeros_like(top)], axis=1), jnp.concatenate([corner, bottom], axis=1)], axis=0
    )


def factor_inverse(s_ref, z_ref, m_ref):
    n = s_ref.shape[0]
    size = 2 * BASE
    row = lax.broadcasted_iota(jnp.int32, (n, n), 0)
    col = lax.broadcasted_iota(jnp.int32, (n, n), 1)
    z_ref[...] = jnp.where(row == col, 1.0, 0.0).astype(jnp.float32)

    def step(k, carry):
        here = pl.ds(pl.multiple_of(k * size, size), size)
        inverse = split(pair_inverse(s_ref[here, here]))
        us = split(dot3(inverse, split(s_ref[here, :])))
        uz = dot3(inverse, split(z_ref[here, :]))
        m_ref[here, :] = uz
        uz = split(uz)
        s_ref[...] -= dot3(us, us, ((0,), (0,)))
        z_ref[...] -= dot3(us, uz, ((0,), (0,)))
        return carry

    lax.fori_loop(0, n // size, step, 0)


AXES = ("prow", "pcol")
NB = 256
NEWEST = 63
PLANES = 8
CHUNK = 2 * NB // PLANES
HALF = CHUNK // 2
LANES = 128
VMEM = pl.BlockSpec(memory_space=pltpu.VMEM)
SMEM = pl.BlockSpec(memory_space=pltpu.SMEM)
ROW, COLUMN, ROOT, HELD, FLIPPED, FIRST, SECOND = range(7)
MASKS = (0, 4, 2, 6, 1, 5, 3, 7)
PARAMS = pltpu.CompilerParams(vmem_limit_bytes=48 * 1024 * 1024)


def chunk_of(info, plane):
    return plane // 2 + PLANES // 2 * ((plane + info[ROOT]) % 2)


def place_of(info, plane):
    return (chunk_of(info, plane) + PLANES // 2 * info[FLIPPED]) % PLANES


def block_column(ref, t, rows):
    return jnp.concatenate([ref[pl.ds(2 * t + j, rows, stride=4), :] for j in range(2)], axis=1)


def pick_kernel(info, piece_ref, both_ref):
    both_ref[:, :NB] = block_column(piece_ref, info[HELD], CHUNK)
    both_ref[:, NB:] = block_column(piece_ref, 1, CHUNK)


def pick(info, piece):
    return pl.pallas_call(
        pick_kernel,
        out_shape=jax.ShapeDtypeStruct((CHUNK, 2 * NB), jnp.float32),
        in_specs=[SMEM, VMEM],
        out_specs=VMEM,
        compiler_params=PARAMS,
        name="pick",
    )(info, piece)


def first_kernel(info, own_ref, twin_ref, m_ref, w_ref, rest_ref, d_ref, s_ref, z_ref):
    flip = info[FLIPPED] == 1
    core = info[COLUMN] % 2
    for slot in range(PLANES):
        base = place_of(info, info[ROW] ^ MASKS[slot]) * CHUNK
        for ref, side in ((own_ref, core), (twin_ref, 1 - core)):
            v = ref[slot]
            v = jnp.where(flip, jnp.concatenate([v[:, NB:], v[:, :NB]], axis=1), v)
            d_ref[pl.ds(pl.multiple_of(base + side * HALF, HALF), HALF), :] = v
    s_ref[...] = d_ref[:NB, :NB]
    factor_inverse(s_ref, z_ref, m_ref)
    inverse = split(m_ref[...])
    below = split(dot3(split(d_ref[NB:, :NB]), inverse, ((1,), (1,))))
    rest_ref[...] = d_ref[NB:, NB:] - dot3(below, below, ((1,), (1,)))
    w_ref[...] = dot3(below, inverse)


def second_kernel(w_ref, rest_ref, m_ref, corner_ref, s_ref, z_ref):
    s_ref[...] = rest_ref[...]
    factor_inverse(s_ref, z_ref, m_ref)
    corner_ref[...] = -product(m_ref[...], w_ref[...])


def stage(kernel, name, inputs, outputs, scratch):
    square = lambda: jax.ShapeDtypeStruct((NB, NB), jnp.float32)
    return pl.pallas_call(
        kernel,
        out_shape=[square() for _ in range(outputs)],
        in_specs=inputs,
        out_specs=[VMEM] * outputs,
        scratch_shapes=scratch + [pltpu.VMEM((NB, NB), jnp.float32)] * 2,
        compiler_params=PARAMS,
        cost_estimate=pl.CostEstimate(flops=10**8, transcendentals=0, bytes_accessed=4 * 10**7),
        name=name,
    )


def first_factor(info, own, twin):
    whole = [pltpu.VMEM((2 * NB, 2 * NB), jnp.float32)]
    return stage(first_kernel, "first", [SMEM, VMEM, VMEM], 3, whole)(info, own, twin)


def second_factor(carried, rest):
    return stage(second_kernel, "second", [VMEM, VMEM], 2, [])(carried, rest)


def cross_kernel(info, first_ref, second_ref, corner_ref, near_ref, far_ref, w_ref, c_ref, t_ref, x_ref):
    t_ref[:NB, :NB] = first_ref[...].T
    t_ref[:NB, NB:] = corner_ref[...].T
    t_ref[NB:, :NB] = jnp.zeros((NB, NB), jnp.float32)
    t_ref[NB:, NB:] = second_ref[...].T
    for plane in range(PLANES):
        start = pl.multiple_of(place_of(info, plane) * CHUNK, CHUNK)
        x_ref[plane * CHUNK : (plane + 1) * CHUNK, :] = t_ref[pl.ds(start, CHUNK), :]
    weights = split(x_ref[...])
    w_ref[...] = stack(weights)
    high, low = weights[0].T, weights[1].T
    for slot in range(PLANES):
        ref = (near_ref, far_ref)[slot // 4].at[slot % 4]
        start = pl.multiple_of((info[ROW] ^ MASKS[slot]) * CHUNK, CHUNK)
        for column in range(2):
            x_ref[pl.ds(start, CHUNK), column * NB : (column + 1) * NB] = block_column(ref, column, CHUNK)
    rows = jnp.concatenate([high, high, low], axis=1)
    c_ref[...] = stack(split(jnp.dot(rows, stack(split(x_ref[...])), preferred_element_type=jnp.float32)))


def cross(info, first, second, corner, near, far):
    n = 2 * NB
    return pl.pallas_call(
        cross_kernel,
        out_shape=[jax.ShapeDtypeStruct((3 * n, n), jnp.bfloat16)] * 2,
        in_specs=[SMEM] + [VMEM] * 5,
        out_specs=[VMEM] * 2,
        scratch_shapes=[pltpu.VMEM((n, n), jnp.float32)] * 2,
        compiler_params=PARAMS,
        name="cross",
    )(info, first, second, corner, near, far)


def update_kernel(info, w_ref, c_ref, g_ref, a_ref, panels_ref, t_ref):
    group = pl.program_id(0)
    first, second = info[FIRST], info[SECOND]
    for t in range(2):
        block = (t * pl.num_programs(0) + group) * PLANES + info[ROW]
        columns = jnp.concatenate([block_column(g_ref.at[plane], t, CHUNK) for plane in range(PLANES)], axis=0)
        rows = stacked(columns.T, w_ref[...])
        row_kept = (block != first) & (block != second)
        panels_ref[0, t, 0] = rows[:, :NB]
        panels_ref[1, t, 0] = jnp.where(block != first, rows[:, NB:], 0.0)
        trail = stacked(rows, c_ref[...])
        for column in range(2):
            number = info[COLUMN] + 32 * column
            kept = row_kept & (number != first) & (number != second)
            for j in range(2):
                where = pl.ds(2 * column + j, NB, stride=4)
                start = column * NB + j * LANES
                t_ref[t, 0, where, :] = jnp.where(kept, a_ref[t, 0, where, :] - trail[:, start : start + LANES], 0.0)


def update(info, factors, gathered, flat):
    br, rows, _ = flat.shape
    groups = gathered.shape[0] // PLANES
    block = lambda k, info: (0, k, 0, 0)
    return pl.pallas_call(
        update_kernel,
        grid_spec=pltpu.PrefetchScalarGridSpec(
            num_scalar_prefetch=1,
            grid=(groups,),
            in_specs=[VMEM] * 2
            + [
                pl.BlockSpec((PLANES, 4 * CHUNK, LANES), lambda k, info: (k, 0, 0)),
                pl.BlockSpec((2, 1, rows, LANES), block),
            ],
            out_specs=[
                pl.BlockSpec((2, 2, 1, NB, NB), lambda k, info: (0, 0, k, 0, 0)),
                pl.BlockSpec((2, 1, rows, LANES), block),
            ],
        ),
        out_shape=[
            jax.ShapeDtypeStruct((2, 2, groups, NB, NB), jnp.float32),
            jax.ShapeDtypeStruct((2, groups) + flat.shape[1:], jnp.float32),
        ],
        compiler_params=PARAMS,
        name="update",
    )(info, *factors, gathered, flat.reshape((2, groups) + flat.shape[1:]))


def shards(kernel, pivots):
    height, width = lax.axis_size("prow"), lax.axis_size("pcol")
    assert (height, width) == (PLANES, 32)
    br, bc = kernel.shape[0], kernel.shape[3]
    assert bc == 2
    flat = kernel.reshape(br, NB * bc * NB // LANES, LANES)
    r = lax.axis_index("prow")
    c = lax.axis_index("pcol")
    flipped = pivots[0] == NEWEST
    other = jnp.where(flipped, pivots[1], pivots[0])
    block_row, root_row = other >> 3, other & 7
    root_t, root_col = other >> 5, other & 31
    info = jnp.stack([r, c, root_row, root_t, flipped.astype(jnp.int32), pivots[0], pivots[1]])
    device = lambda row, column: row * width + column
    everyone = [(row, column) for row in range(height) for column in range(width)]
    send = lambda value, to: lax.ppermute(value, AXES, [(device(a, b), device(*to(a, b))) for a, b in everyone])
    double = lambda value, mask: jnp.concatenate([value, send(value, lambda a, b: (a ^ mask, b))], axis=0)
    tie = lambda *values: lax.optimization_barrier(values)
    core_twin = lambda value: send(value, lambda a, b: (a, b ^ 1))

    piece_rows = 4 * CHUNK
    part = lambda rows, q: rows[q * piece_rows : (q + 1) * piece_rows]
    line = lambda start, end: [(device(start, k), device(end, k)) for k in range(width)]

    def scatter_from(root):
        parity, quarter = root % 2, root // 2
        away = 1 - parity

        def run(others, newest):
            arrived = []
            for q in range(4):
                plane = 2 * q + away
                if plane != height - 1:
                    arrived.append((plane, lax.ppermute(part(newest, q), AXES, line(height - 1, plane))))
                if q != quarter:
                    plane = 2 * q + parity
                    pairs = line(root, plane)
                    if quarter in (1, 2):
                        pairs = line(2 * quarter, 2 * q) + line(2 * quarter + 1, 2 * q + 1)
                    arrived.append((plane, lax.ppermute(part(others, q), AXES, pairs)))
            arrived.append((root, part(others, quarter)))
            if away == 1:
                arrived.append((height - 1, part(newest, 3)))
            piece = arrived[0][1]
            for plane, value in arrived[1:]:
                piece = jnp.where(r == plane, value, piece)
            return piece

        return run

    others = lax.dynamic_slice(flat, (block_row, 0, 0), (1,) + flat.shape[1:])[0]
    rows = tie(others, flat[NEWEST // height])
    piece = lax.switch(root_row, [scatter_from(root) for root in range(height)], *rows)
    both = pick(info, piece)

    moved = send(piece, lambda a, b: (b % height, (b // height) * height + a))

    crossing = double(piece[None], 4)

    core, ypos, xpos = c & 1, (c >> 1) & 3, c >> 3
    rcore, ry, rx = root_col & 1, (root_col >> 1) & 3, root_col >> 3
    side = lax.broadcasted_iota(jnp.int32, (CHUNK, 2 * NB), 1) < NB
    both = jnp.where(jnp.where(side, core == rcore, core == 1), both, core_twin(both))
    mine = lax.dynamic_slice_in_dim(both, core * HALF, HALF, 0)
    side = side[:HALF]

    def spread(value, position, goal, last, shift):
        source = jnp.where(side, position ^ goal, position ^ last)
        out = value
        for d in range(1, 4):
            out = jnp.where(source == d, send(value, lambda a, b: (a, b ^ (d << shift))), out)
        return out

    mine = spread(mine, xpos, rx, 3, 3)
    moved, crossing, mine = tie(moved, crossing, mine)
    gathered = lax.all_gather(moved, "pcol", axis=0, tiled=False)
    mine = spread(mine, ypos, ry, 3, 1)
    ring = double(double(double(mine[None], 4), 2), 1)
    crossing, ring = tie(crossing, ring)
    facing = send(crossing, lambda a, b: (a ^ 2, b))
    first, carried, rest = first_factor(info, ring, core_twin(ring))
    crossing, facing, carried, rest = tie(crossing, facing, carried, rest)
    crossing = jnp.concatenate([crossing, facing], axis=0)
    beyond = send(crossing, lambda a, b: (a ^ 1, b))
    second, corner = second_factor(carried, rest)
    factors = cross(info, first, second, corner, crossing, beyond)
    panels, trailing = update(info, factors, gathered, flat)
    return panels.reshape(2, br, 1, NB, NB), trailing.reshape(kernel.shape)


def solution(mesh):
    in_specs = (P(None, "prow", None, None, "pcol", None), P())
    out_specs = (P(None, None, "prow", None, None), P(None, "prow", None, None, "pcol", None))
    return jax.shard_map(shards, mesh=mesh, in_specs=in_specs, out_specs=out_specs, check_vma=False)
```

```python
import jax
import jax.numpy as jnp
from jax import lax
from jax.experimental import pallas as pl
from jax.experimental.pallas import tpu as pltpu
from jax.sharding import PartitionSpec as P

BASE = 64
GROUP = 8


def split(v):
    high = v.astype(jnp.bfloat16)
    low = (v - high.astype(jnp.float32)).astype(jnp.bfloat16)
    return high, low


def dot3(a, b, dims=((1,), (0,))):
    (ah, al), (bh, bl) = a, b
    f = lambda u, v: lax.dot_general(u, v, (dims, ((), ())), preferred_element_type=jnp.float32)
    return f(ah, bh) + (f(ah, bl) + f(al, bh))


def stack(b):
    return jnp.concatenate([b[0], b[1], b[0]], axis=0)


def stacked(a, b):
    high, low = split(a)
    return jnp.dot(jnp.concatenate([high, high, low], axis=1), b, preferred_element_type=jnp.float32)


def product(a, b, dims=((1,), (0,))):
    return dot3(split(a), split(b), dims)


def factor_group(scalars):
    n = GROUP
    g = [row[:] for row in scalars]
    unit = [[None] * n for _ in range(n)]
    pivots, inverses = [], []
    for q in range(0, n, 2):
        a, b, d = g[q][q], g[q + 1][q], g[q + 1][q + 1]
        det = a * d - b * b
        over = 1.0 / det
        inv = 1.0 / a
        step = b * inv
        below = d - step * b
        pivots += [a, below]
        inverses += [inv, a * over]
        unit[q + 1][q] = step
        for i in range(q + 2, n):
            x, y = g[i][q], g[i][q + 1]
            unit[i][q] = x * inv
            unit[i][q + 1] = (y * a - x * b) * over
        for i in range(q + 2, n):
            x, y = g[i][q], g[i][q + 1]
            u, v = (x * d - y * b) * over, unit[i][q + 1]
            for k in range(q + 2, i + 1):
                g[i][k] = g[i][k] - (u * g[k][q] + v * g[k][q + 1])
    w = [[None] * n for _ in range(n)]
    for q in range(n):
        for i in range(q + 1, n):
            acc = unit[i][q]
            for k in range(q + 1, i):
                acc = acc + unit[i][k] * w[k][q]
            w[i][q] = -acc
    return w, pivots, inverses


def base_inverse(s):
    lanes = 2 * BASE
    row = lax.broadcasted_iota(jnp.int32, (BASE, BASE), 0)
    col = lax.broadcasted_iota(jnp.int32, (BASE, BASE), 1)
    eye = jnp.where(row == col, 1.0, 0.0).astype(jnp.float32)
    table = jnp.concatenate([s, eye], axis=1)
    groups = [table[GROUP * h : GROUP * h + GROUP, :] for h in range(BASE // GROUP)]
    shape = (GROUP, lanes)
    sub = lax.broadcasted_iota(jnp.int32, shape, 0)
    spread = lambda v: jnp.broadcast_to(v, shape)
    done = []
    for g in range(BASE // GROUP):
        p = groups[g]
        start = GROUP * g
        cols = [spread(p[:, start + q : start + q + 1]) for q in range(GROUP)]
        scalars = [[spread(cols[q][i : i + 1, :]) if i >= q else None for q in range(GROUP)] for i in range(GROUP)]
        w, pivots, inverses = factor_group(scalars)
        rows = [spread(p[q : q + 1, :]) for q in range(GROUP)]
        reduced = []
        for i in range(GROUP):
            acc = rows[i]
            for q in range(i):
                acc = acc + w[i][q] * rows[q]
            reduced.append(acc)
        for h in range(g + 1, BASE // GROUP):
            t = groups[h]
            cb = [spread(t[:, start + q : start + q + 1]) for q in range(GROUP)]
            for q in range(GROUP):
                v = cb[q]
                for k in range(q):
                    v = v + w[q][k] * cb[k]
                t = t - (v * inverses[q]) * reduced[q]
            groups[h] = t
        out = jnp.zeros(shape, jnp.float32)
        for q in range(GROUP):
            out = jnp.where(sub == q, reduced[q] * lax.rsqrt(pivots[q]), out)
        done.append(out)
    return jnp.concatenate(done, axis=0)[:, BASE:]


def pair_inverse(s):
    top = base_inverse(s[:BASE, :BASE])
    below = product(s[BASE:, :BASE], top, ((1,), (1,)))
    rest = s[BASE:, BASE:] - product(below, below, ((1,), (1,)))
    carried = product(below, top)
    bottom = base_inverse(rest)
    corner = -product(bottom, carried)
    return jnp.concatenate(
        [jnp.concatenate([top, jnp.zeros_like(top)], axis=1), jnp.concatenate([corner, bottom], axis=1)], axis=0
    )


def factor_inverse(s_ref, z_ref, m_ref):
    n = s_ref.shape[0]
    size = 2 * BASE
    row = lax.broadcasted_iota(jnp.int32, (n, n), 0)
    col = lax.broadcasted_iota(jnp.int32, (n, n), 1)
    z_ref[...] = jnp.where(row == col, 1.0, 0.0).astype(jnp.float32)

    def step(k, carry):
        here = pl.ds(pl.multiple_of(k * size, size), size)
        inverse = split(pair_inverse(s_ref[here, here]))
        us = split(dot3(inverse, split(s_ref[here, :])))
        uz = dot3(inverse, split(z_ref[here, :]))
        m_ref[here, :] = uz
        uz = split(uz)
        s_ref[...] -= dot3(us, us, ((0,), (0,)))
        z_ref[...] -= dot3(us, uz, ((0,), (0,)))
        return carry

    lax.fori_loop(0, n // size, step, 0)


AXES = ("prow", "pcol")
NB = 256
NEWEST = 63
PLANES = 8
CHUNK = 2 * NB // PLANES
HALF = CHUNK // 2
LANES = 128
VMEM = pl.BlockSpec(memory_space=pltpu.VMEM)
SMEM = pl.BlockSpec(memory_space=pltpu.SMEM)
ROW, COLUMN, ROOT, HELD, FLIPPED, FIRST, SECOND = range(7)
MASKS = (0, 4, 2, 6, 1, 5, 3, 7)
PARAMS = pltpu.CompilerParams(vmem_limit_bytes=48 * 1024 * 1024)


def chunk_of(info, plane):
    return plane // 2 + PLANES // 2 * ((plane + info[ROOT]) % 2)


def place_of(info, plane):
    return (chunk_of(info, plane) + PLANES // 2 * info[FLIPPED]) % PLANES


def block_column(ref, t, rows):
    return jnp.concatenate([ref[pl.ds(2 * t + j, rows, stride=4), :] for j in range(2)], axis=1)


def pick_kernel(info, piece_ref, both_ref):
    both_ref[:, :NB] = block_column(piece_ref, info[HELD], CHUNK)
    both_ref[:, NB:] = block_column(piece_ref, 1, CHUNK)


def pick(info, piece):
    return pl.pallas_call(
        pick_kernel,
        out_shape=jax.ShapeDtypeStruct((CHUNK, 2 * NB), jnp.float32),
        in_specs=[SMEM, VMEM],
        out_specs=VMEM,
        compiler_params=PARAMS,
        name="pick",
    )(info, piece)


def first_kernel(info, own_ref, twin_ref, m_ref, w_ref, rest_ref, d_ref, s_ref, z_ref):
    flip = info[FLIPPED] == 1
    core = info[COLUMN] % 2
    for slot in range(PLANES):
        base = place_of(info, info[ROW] ^ MASKS[slot]) * CHUNK
        for ref, side in ((own_ref, core), (twin_ref, 1 - core)):
            v = ref[slot]
            v = jnp.where(flip, jnp.concatenate([v[:, NB:], v[:, :NB]], axis=1), v)
            d_ref[pl.ds(pl.multiple_of(base + side * HALF, HALF), HALF), :] = v
    s_ref[...] = d_ref[:NB, :NB]
    factor_inverse(s_ref, z_ref, m_ref)
    inverse = split(m_ref[...])
    below = split(dot3(split(d_ref[NB:, :NB]), inverse, ((1,), (1,))))
    rest_ref[...] = d_ref[NB:, NB:] - dot3(below, below, ((1,), (1,)))
    w_ref[...] = dot3(below, inverse)


def second_kernel(w_ref, rest_ref, m_ref, corner_ref, s_ref, z_ref):
    s_ref[...] = rest_ref[...]
    factor_inverse(s_ref, z_ref, m_ref)
    corner_ref[...] = -product(m_ref[...], w_ref[...])


def stage(kernel, name, inputs, outputs, scratch):
    square = lambda: jax.ShapeDtypeStruct((NB, NB), jnp.float32)
    return pl.pallas_call(
        kernel,
        out_shape=[square() for _ in range(outputs)],
        in_specs=inputs,
        out_specs=[VMEM] * outputs,
        scratch_shapes=scratch + [pltpu.VMEM((NB, NB), jnp.float32)] * 2,
        compiler_params=PARAMS,
        cost_estimate=pl.CostEstimate(flops=10**8, transcendentals=0, bytes_accessed=4 * 10**7),
        name=name,
    )


def first_factor(info, own, twin):
    whole = [pltpu.VMEM((2 * NB, 2 * NB), jnp.float32)]
    return stage(first_kernel, "first", [SMEM, VMEM, VMEM], 3, whole)(info, own, twin)


def second_factor(carried, rest):
    return stage(second_kernel, "second", [VMEM, VMEM], 2, [])(carried, rest)


def cross_kernel(info, first_ref, second_ref, corner_ref, near_ref, far_ref, w_ref, c_ref, t_ref, x_ref):
    t_ref[:NB, :NB] = first_ref[...].T
    t_ref[:NB, NB:] = corner_ref[...].T
    t_ref[NB:, :NB] = jnp.zeros((NB, NB), jnp.float32)
    t_ref[NB:, NB:] = second_ref[...].T
    for plane in range(PLANES):
        start = pl.multiple_of(place_of(info, plane) * CHUNK, CHUNK)
        x_ref[plane * CHUNK : (plane + 1) * CHUNK, :] = t_ref[pl.ds(start, CHUNK), :]
    weights = split(x_ref[...])
    w_ref[...] = stack(weights)
    high, low = weights[0].T, weights[1].T
    for slot in range(PLANES):
        ref = (near_ref, far_ref)[slot // 4].at[slot % 4]
        start = pl.multiple_of((info[ROW] ^ MASKS[slot]) * CHUNK, CHUNK)
        for column in range(2):
            x_ref[pl.ds(start, CHUNK), column * NB : (column + 1) * NB] = block_column(ref, column, CHUNK)
    rows = jnp.concatenate([high, high, low], axis=1)
    c_ref[...] = stack(split(jnp.dot(rows, stack(split(x_ref[...])), preferred_element_type=jnp.float32)))


def cross(info, first, second, corner, near, far):
    n = 2 * NB
    return pl.pallas_call(
        cross_kernel,
        out_shape=[jax.ShapeDtypeStruct((3 * n, n), jnp.bfloat16)] * 2,
        in_specs=[SMEM] + [VMEM] * 5,
        out_specs=[VMEM] * 2,
        scratch_shapes=[pltpu.VMEM((n, n), jnp.float32)] * 2,
        compiler_params=PARAMS,
        name="cross",
    )(info, first, second, corner, near, far)


def update_kernel(info, w_ref, c_ref, g_ref, a_ref, panels_ref, t_ref):
    group = pl.program_id(0)
    first, second = info[FIRST], info[SECOND]
    for t in range(2):
        block = (t * pl.num_programs(0) + group) * PLANES + info[ROW]
        columns = jnp.concatenate([block_column(g_ref.at[plane], t, CHUNK) for plane in range(PLANES)], axis=0)
        rows = stacked(columns.T, w_ref[...])
        row_kept = (block != first) & (block != second)
        panels_ref[0, t, 0] = rows[:, :NB]
        panels_ref[1, t, 0] = jnp.where(block != first, rows[:, NB:], 0.0)
        trail = stacked(rows, c_ref[...])
        for column in range(2):
            number = info[COLUMN] + 32 * column
            kept = row_kept & (number != first) & (number != second)
            for j in range(2):
                where = pl.ds(2 * column + j, NB, stride=4)
                start = column * NB + j * LANES
                t_ref[t, 0, where, :] = jnp.where(kept, a_ref[t, 0, where, :] - trail[:, start : start + LANES], 0.0)


def update(info, factors, gathered, flat):
    br, rows, _ = flat.shape
    groups = gathered.shape[0] // PLANES
    block = lambda k, info: (0, k, 0, 0)
    return pl.pallas_call(
        update_kernel,
        grid_spec=pltpu.PrefetchScalarGridSpec(
            num_scalar_prefetch=1,
            grid=(groups,),
            in_specs=[VMEM] * 2
            + [
                pl.BlockSpec((PLANES, 4 * CHUNK, LANES), lambda k, info: (k, 0, 0)),
                pl.BlockSpec((2, 1, rows, LANES), block),
            ],
            out_specs=[
                pl.BlockSpec((2, 2, 1, NB, NB), lambda k, info: (0, 0, k, 0, 0)),
                pl.BlockSpec((2, 1, rows, LANES), block),
            ],
        ),
        out_shape=[
            jax.ShapeDtypeStruct((2, 2, groups, NB, NB), jnp.float32),
            jax.ShapeDtypeStruct((2, groups) + flat.shape[1:], jnp.float32),
        ],
        compiler_params=PARAMS,
        name="update",
    )(info, *factors, gathered, flat.reshape((2, groups) + flat.shape[1:]))


def shards(kernel, pivots):
    height, width = lax.axis_size("prow"), lax.axis_size("pcol")
    assert (height, width) == (PLANES, 32)
    br, bc = kernel.shape[0], kernel.shape[3]
    assert bc == 2
    flat = kernel.reshape(br, NB * bc * NB // LANES, LANES)
    r = lax.axis_index("prow")
    c = lax.axis_index("pcol")
    flipped = pivots[0] == NEWEST
    other = jnp.where(flipped, pivots[1], pivots[0])
    block_row, root_row = other >> 3, other & 7
    root_t, root_col = other >> 5, other & 31
    info = jnp.stack([r, c, root_row, root_t, flipped.astype(jnp.int32), pivots[0], pivots[1]])
    device = lambda row, column: row * width + column
    everyone = [(row, column) for row in range(height) for column in range(width)]
    send = lambda value, to: lax.ppermute(value, AXES, [(device(a, b), device(*to(a, b))) for a, b in everyone])
    double = lambda value, mask: jnp.concatenate([value, send(value, lambda a, b: (a ^ mask, b))], axis=0)
    tie = lambda *values: lax.optimization_barrier(values)
    core_twin = lambda value: send(value, lambda a, b: (a, b ^ 1))

    piece_rows = 4 * CHUNK
    part = lambda rows, q: rows[q * piece_rows : (q + 1) * piece_rows]
    line = lambda start, end: [(device(start, k), device(end, k)) for k in range(width)]

    def scatter_from(root):
        parity, quarter = root % 2, root // 2
        away = 1 - parity

        def run(others, newest):
            arrived = []
            for q in range(4):
                plane = 2 * q + away
                if plane != height - 1:
                    arrived.append((plane, lax.ppermute(part(newest, q), AXES, line(height - 1, plane))))
                if q != quarter:
                    plane = 2 * q + parity
                    pairs = line(root, plane)
                    if quarter in (1, 2):
                        pairs = line(2 * quarter, 2 * q) + line(2 * quarter + 1, 2 * q + 1)
                    arrived.append((plane, lax.ppermute(part(others, q), AXES, pairs)))
            arrived.append((root, part(others, quarter)))
            if away == 1:
                arrived.append((height - 1, part(newest, 3)))
            piece = arrived[0][1]
            for plane, value in arrived[1:]:
                piece = jnp.where(r == plane, value, piece)
            return piece

        return run

    others = lax.dynamic_slice(flat, (block_row, 0, 0), (1,) + flat.shape[1:])[0]
    rows = tie(others, flat[NEWEST // height])
    piece = lax.switch(root_row, [scatter_from(root) for root in range(height)], *rows)
    both = pick(info, piece)

    moved = send(piece, lambda a, b: (b % height, (b // height) * height + a))

    crossing = double(piece[None], 4)

    core, ypos, xpos = c & 1, (c >> 1) & 3, c >> 3
    rcore, ry, rx = root_col & 1, (root_col >> 1) & 3, root_col >> 3
    side = lax.broadcasted_iota(jnp.int32, (CHUNK, 2 * NB), 1) < NB
    both = jnp.where(jnp.where(side, core == rcore, core == 1), both, core_twin(both))
    mine = lax.dynamic_slice_in_dim(both, core * HALF, HALF, 0)
    side = side[:HALF]

    def spread(value, position, goal, last, shift):
        source = jnp.where(side, position ^ goal, position ^ last)
        out = value
        for d in range(1, 4):
            out = jnp.where(source == d, send(value, lambda a, b: (a, b ^ (d << shift))), out)
        return out

    mine = spread(mine, xpos, rx, 3, 3)
    mine = spread(mine, ypos, ry, 3, 1)
    moved, mine = tie(moved, mine)
    gathered = lax.all_gather(moved, "pcol", axis=0, tiled=False)
    ring = double(double(double(mine[None], 4), 2), 1)
    crossing, ring = tie(crossing, ring)
    facing = send(crossing, lambda a, b: (a ^ 2, b))
    first, carried, rest = first_factor(info, ring, core_twin(ring))
    crossing, facing, carried, rest = tie(crossing, facing, carried, rest)
    crossing = jnp.concatenate([crossing, facing], axis=0)
    beyond = send(crossing, lambda a, b: (a ^ 1, b))
    second, corner = second_factor(carried, rest)
    factors = cross(info, first, second, corner, crossing, beyond)
    panels, trailing = update(info, factors, gathered, flat)
    return panels.reshape(2, br, 1, NB, NB), trailing.reshape(kernel.shape)


def solution(mesh):
    in_specs = (P(None, "prow", None, None, "pcol", None), P())
    out_specs = (P(None, None, "prow", None, None), P(None, "prow", None, None, "pcol", None))
    return jax.shard_map(shards, mesh=mesh, in_specs=in_specs, out_specs=out_specs, check_vma=False)
```

```python
import jax
import jax.numpy as jnp
from jax import lax
from jax.experimental import pallas as pl
from jax.experimental.pallas import tpu as pltpu
from jax.sharding import PartitionSpec as P

BASE = 64
GROUP = 8


def split(v):
    high = v.astype(jnp.bfloat16)
    low = (v - high.astype(jnp.float32)).astype(jnp.bfloat16)
    return high, low


def dot3(a, b, dims=((1,), (0,))):
    (ah, al), (bh, bl) = a, b
    f = lambda u, v: lax.dot_general(u, v, (dims, ((), ())), preferred_element_type=jnp.float32)
    return f(ah, bh) + (f(ah, bl) + f(al, bh))


def stack(b):
    return jnp.concatenate([b[0], b[1], b[0]], axis=0)


def stacked(a, b):
    high, low = split(a)
    return jnp.dot(jnp.concatenate([high, high, low], axis=1), b, preferred_element_type=jnp.float32)


def product(a, b, dims=((1,), (0,))):
    return dot3(split(a), split(b), dims)


def factor_group(scalars):
    n = GROUP
    g = [row[:] for row in scalars]
    unit = [[None] * n for _ in range(n)]
    pivots, inverses = [], []
    for q in range(0, n, 2):
        a, b, d = g[q][q], g[q + 1][q], g[q + 1][q + 1]
        det = a * d - b * b
        over = 1.0 / det
        inv = 1.0 / a
        step = b * inv
        below = d - step * b
        pivots += [a, below]
        inverses += [inv, a * over]
        unit[q + 1][q] = step
        for i in range(q + 2, n):
            x, y = g[i][q], g[i][q + 1]
            unit[i][q] = x * inv
            unit[i][q + 1] = (y * a - x * b) * over
        for i in range(q + 2, n):
            x, y = g[i][q], g[i][q + 1]
            u, v = (x * d - y * b) * over, unit[i][q + 1]
            for k in range(q + 2, i + 1):
                g[i][k] = g[i][k] - (u * g[k][q] + v * g[k][q + 1])
    w = [[None] * n for _ in range(n)]
    for q in range(n):
        for i in range(q + 1, n):
            acc = unit[i][q]
            for k in range(q + 1, i):
                acc = acc + unit[i][k] * w[k][q]
            w[i][q] = -acc
    return w, pivots, inverses


def base_inverse(s):
    lanes = 2 * BASE
    row = lax.broadcasted_iota(jnp.int32, (BASE, BASE), 0)
    col = lax.broadcasted_iota(jnp.int32, (BASE, BASE), 1)
    eye = jnp.where(row == col, 1.0, 0.0).astype(jnp.float32)
    table = jnp.concatenate([s, eye], axis=1)
    groups = [table[GROUP * h : GROUP * h + GROUP, :] for h in range(BASE // GROUP)]
    shape = (GROUP, lanes)
    sub = lax.broadcasted_iota(jnp.int32, shape, 0)
    spread = lambda v: jnp.broadcast_to(v, shape)
    done = []
    for g in range(BASE // GROUP):
        p = groups[g]
        start = GROUP * g
        cols = [spread(p[:, start + q : start + q + 1]) for q in range(GROUP)]
        scalars = [[spread(cols[q][i : i + 1, :]) if i >= q else None for q in range(GROUP)] for i in range(GROUP)]
        w, pivots, inverses = factor_group(scalars)
        rows = [spread(p[q : q + 1, :]) for q in range(GROUP)]
        reduced = []
        for i in range(GROUP):
            acc = rows[i]
            for q in range(i):
                acc = acc + w[i][q] * rows[q]
            reduced.append(acc)
        for h in range(g + 1, BASE // GROUP):
            t = groups[h]
            cb = [spread(t[:, start + q : start + q + 1]) for q in range(GROUP)]
            for q in range(GROUP):
                v = cb[q]
                for k in range(q):
                    v = v + w[q][k] * cb[k]
                t = t - (v * inverses[q]) * reduced[q]
            groups[h] = t
        out = jnp.zeros(shape, jnp.float32)
        for q in range(GROUP):
            out = jnp.where(sub == q, reduced[q] * lax.rsqrt(pivots[q]), out)
        done.append(out)
    return jnp.concatenate(done, axis=0)[:, BASE:]


def pair_inverse(s):
    top = base_inverse(s[:BASE, :BASE])
    below = product(s[BASE:, :BASE], top, ((1,), (1,)))
    rest = s[BASE:, BASE:] - product(below, below, ((1,), (1,)))
    carried = product(below, top)
    bottom = base_inverse(rest)
    corner = -product(bottom, carried)
    return jnp.concatenate(
        [jnp.concatenate([top, jnp.zeros_like(top)], axis=1), jnp.concatenate([corner, bottom], axis=1)], axis=0
    )


def factor_inverse(s_ref, z_ref, m_ref):
    n = s_ref.shape[0]
    size = 2 * BASE
    row = lax.broadcasted_iota(jnp.int32, (n, n), 0)
    col = lax.broadcasted_iota(jnp.int32, (n, n), 1)
    z_ref[...] = jnp.where(row == col, 1.0, 0.0).astype(jnp.float32)

    def step(k, carry):
        here = pl.ds(pl.multiple_of(k * size, size), size)
        inverse = split(pair_inverse(s_ref[here, here]))
        us = split(dot3(inverse, split(s_ref[here, :])))
        uz = dot3(inverse, split(z_ref[here, :]))
        m_ref[here, :] = uz
        uz = split(uz)
        s_ref[...] -= dot3(us, us, ((0,), (0,)))
        z_ref[...] -= dot3(us, uz, ((0,), (0,)))
        return carry

    lax.fori_loop(0, n // size, step, 0)


AXES = ("prow", "pcol")
NB = 256
NEWEST = 63
PLANES = 8
CHUNK = 2 * NB // PLANES
HALF = CHUNK // 2
LANES = 128
VMEM = pl.BlockSpec(memory_space=pltpu.VMEM)
SMEM = pl.BlockSpec(memory_space=pltpu.SMEM)
ROW, COLUMN, ROOT, HELD, FLIPPED, FIRST, SECOND = range(7)
MASKS = (0, 4, 2, 6, 1, 5, 3, 7)
PARAMS = pltpu.CompilerParams(vmem_limit_bytes=48 * 1024 * 1024)


def chunk_of(info, plane):
    return plane // 2 + PLANES // 2 * ((plane + info[ROOT]) % 2)


def place_of(info, plane):
    return (chunk_of(info, plane) + PLANES // 2 * info[FLIPPED]) % PLANES


def block_column(ref, t, rows):
    return jnp.concatenate([ref[pl.ds(2 * t + j, rows, stride=4), :] for j in range(2)], axis=1)


def pick_kernel(info, piece_ref, both_ref):
    both_ref[:, :NB] = block_column(piece_ref, info[HELD], CHUNK)
    both_ref[:, NB:] = block_column(piece_ref, 1, CHUNK)


def pick(info, piece):
    return pl.pallas_call(
        pick_kernel,
        out_shape=jax.ShapeDtypeStruct((CHUNK, 2 * NB), jnp.float32),
        in_specs=[SMEM, VMEM],
        out_specs=VMEM,
        compiler_params=PARAMS,
        name="pick",
    )(info, piece)


def first_kernel(info, own_ref, twin_ref, m_ref, w_ref, rest_ref, d_ref, s_ref, z_ref):
    flip = info[FLIPPED] == 1
    core = info[COLUMN] % 2
    for slot in range(PLANES):
        base = place_of(info, info[ROW] ^ MASKS[slot]) * CHUNK
        for ref, side in ((own_ref, core), (twin_ref, 1 - core)):
            v = ref[slot]
            v = jnp.where(flip, jnp.concatenate([v[:, NB:], v[:, :NB]], axis=1), v)
            d_ref[pl.ds(pl.multiple_of(base + side * HALF, HALF), HALF), :] = v
    s_ref[...] = d_ref[:NB, :NB]
    factor_inverse(s_ref, z_ref, m_ref)
    inverse = split(m_ref[...])
    below = split(dot3(split(d_ref[NB:, :NB]), inverse, ((1,), (1,))))
    rest_ref[...] = d_ref[NB:, NB:] - dot3(below, below, ((1,), (1,)))
    w_ref[...] = dot3(below, inverse)


def second_kernel(w_ref, rest_ref, m_ref, corner_ref, s_ref, z_ref):
    s_ref[...] = rest_ref[...]
    factor_inverse(s_ref, z_ref, m_ref)
    corner_ref[...] = -product(m_ref[...], w_ref[...])


def stage(kernel, name, inputs, outputs, scratch):
    square = lambda: jax.ShapeDtypeStruct((NB, NB), jnp.float32)
    return pl.pallas_call(
        kernel,
        out_shape=[square() for _ in range(outputs)],
        in_specs=inputs,
        out_specs=[VMEM] * outputs,
        scratch_shapes=scratch + [pltpu.VMEM((NB, NB), jnp.float32)] * 2,
        compiler_params=PARAMS,
        cost_estimate=pl.CostEstimate(flops=10**8, transcendentals=0, bytes_accessed=4 * 10**7),
        name=name,
    )


def first_factor(info, own, twin):
    whole = [pltpu.VMEM((2 * NB, 2 * NB), jnp.float32)]
    return stage(first_kernel, "first", [SMEM, VMEM, VMEM], 3, whole)(info, own, twin)


def second_factor(carried, rest):
    return stage(second_kernel, "second", [VMEM, VMEM], 2, [])(carried, rest)


def cross_kernel(info, first_ref, second_ref, corner_ref, near_ref, far_ref, w_ref, c_ref, t_ref, x_ref):
    t_ref[:NB, :NB] = first_ref[...].T
    t_ref[:NB, NB:] = corner_ref[...].T
    t_ref[NB:, :NB] = jnp.zeros((NB, NB), jnp.float32)
    t_ref[NB:, NB:] = second_ref[...].T
    for plane in range(PLANES):
        start = pl.multiple_of(place_of(info, plane) * CHUNK, CHUNK)
        x_ref[plane * CHUNK : (plane + 1) * CHUNK, :] = t_ref[pl.ds(start, CHUNK), :]
    weights = split(x_ref[...])
    w_ref[...] = stack(weights)
    high, low = weights[0].T, weights[1].T
    for slot in range(PLANES):
        ref = (near_ref, far_ref)[slot // 4].at[slot % 4]
        start = pl.multiple_of((info[ROW] ^ MASKS[slot]) * CHUNK, CHUNK)
        for column in range(2):
            x_ref[pl.ds(start, CHUNK), column * NB : (column + 1) * NB] = block_column(ref, column, CHUNK)
    rows = jnp.concatenate([high, high, low], axis=1)
    c_ref[...] = stack(split(jnp.dot(rows, stack(split(x_ref[...])), preferred_element_type=jnp.float32)))


def cross(info, first, second, corner, near, far):
    n = 2 * NB
    return pl.pallas_call(
        cross_kernel,
        out_shape=[jax.ShapeDtypeStruct((3 * n, n), jnp.bfloat16)] * 2,
        in_specs=[SMEM] + [VMEM] * 5,
        out_specs=[VMEM] * 2,
        scratch_shapes=[pltpu.VMEM((n, n), jnp.float32)] * 2,
        compiler_params=PARAMS,
        name="cross",
    )(info, first, second, corner, near, far)


def update_kernel(info, w_ref, c_ref, g_ref, a_ref, panels_ref, t_ref):
    group = pl.program_id(0)
    first, second = info[FIRST], info[SECOND]
    for t in range(2):
        block = (t * pl.num_programs(0) + group) * PLANES + info[ROW]
        columns = jnp.concatenate([block_column(g_ref.at[plane], t, CHUNK) for plane in range(PLANES)], axis=0)
        rows = stacked(columns.T, w_ref[...])
        row_kept = (block != first) & (block != second)
        panels_ref[0, t, 0] = rows[:, :NB]
        panels_ref[1, t, 0] = jnp.where(block != first, rows[:, NB:], 0.0)
        trail = stacked(rows, c_ref[...])
        for column in range(2):
            number = info[COLUMN] + 32 * column
            kept = row_kept & (number != first) & (number != second)
            for j in range(2):
                where = pl.ds(2 * column + j, NB, stride=4)
                start = column * NB + j * LANES
                t_ref[t, 0, where, :] = jnp.where(kept, a_ref[t, 0, where, :] - trail[:, start : start + LANES], 0.0)


def update(info, factors, gathered, flat):
    br, rows, _ = flat.shape
    groups = gathered.shape[0] // PLANES
    block = lambda k, info: (0, k, 0, 0)
    return pl.pallas_call(
        update_kernel,
        grid_spec=pltpu.PrefetchScalarGridSpec(
            num_scalar_prefetch=1,
            grid=(groups,),
            in_specs=[VMEM] * 2
            + [
                pl.BlockSpec((PLANES, 4 * CHUNK, LANES), lambda k, info: (k, 0, 0)),
                pl.BlockSpec((2, 1, rows, LANES), block),
            ],
            out_specs=[
                pl.BlockSpec((2, 2, 1, NB, NB), lambda k, info: (0, 0, k, 0, 0)),
                pl.BlockSpec((2, 1, rows, LANES), block),
            ],
        ),
        out_shape=[
            jax.ShapeDtypeStruct((2, 2, groups, NB, NB), jnp.float32),
            jax.ShapeDtypeStruct((2, groups) + flat.shape[1:], jnp.float32),
        ],
        compiler_params=PARAMS,
        name="update",
    )(info, *factors, gathered, flat.reshape((2, groups) + flat.shape[1:]))


def shards(kernel, pivots):
    height, width = lax.axis_size("prow"), lax.axis_size("pcol")
    assert (height, width) == (PLANES, 32)
    br, bc = kernel.shape[0], kernel.shape[3]
    assert bc == 2
    flat = kernel.reshape(br, NB * bc * NB // LANES, LANES)
    r = lax.axis_index("prow")
    c = lax.axis_index("pcol")
    flipped = pivots[0] == NEWEST
    other = jnp.where(flipped, pivots[1], pivots[0])
    block_row, root_row = other >> 3, other & 7
    root_t, root_col = other >> 5, other & 31
    info = jnp.stack([r, c, root_row, root_t, flipped.astype(jnp.int32), pivots[0], pivots[1]])
    device = lambda row, column: row * width + column
    everyone = [(row, column) for row in range(height) for column in range(width)]
    send = lambda value, to: lax.ppermute(value, AXES, [(device(a, b), device(*to(a, b))) for a, b in everyone])
    double = lambda value, mask: jnp.concatenate([value, send(value, lambda a, b: (a ^ mask, b))], axis=0)
    tie = lambda *values: lax.optimization_barrier(values)
    core_twin = lambda value: send(value, lambda a, b: (a, b ^ 1))

    piece_rows = 4 * CHUNK
    part = lambda rows, q: rows[q * piece_rows : (q + 1) * piece_rows]
    line = lambda start, end: [(device(start, k), device(end, k)) for k in range(width)]

    def scatter_from(root):
        parity, quarter = root % 2, root // 2
        away = 1 - parity

        def run(others, newest):
            arrived = []
            for q in range(4):
                plane = 2 * q + away
                if plane != height - 1:
                    arrived.append((plane, lax.ppermute(part(newest, q), AXES, line(height - 1, plane))))
                if q != quarter:
                    plane = 2 * q + parity
                    pairs = line(root, plane)
                    if quarter in (1, 2):
                        pairs = line(2 * quarter, 2 * q) + line(2 * quarter + 1, 2 * q + 1)
                    arrived.append((plane, lax.ppermute(part(others, q), AXES, pairs)))
            arrived.append((root, part(others, quarter)))
            if away == 1:
                arrived.append((height - 1, part(newest, 3)))
            piece = arrived[0][1]
            for plane, value in arrived[1:]:
                piece = jnp.where(r == plane, value, piece)
            return piece

        return run

    others = lax.dynamic_slice(flat, (block_row, 0, 0), (1,) + flat.shape[1:])[0]
    rows = tie(others, flat[NEWEST // height])
    piece = lax.switch(root_row, [scatter_from(root) for root in range(height)], *rows)
    both = pick(info, piece)

    moved = send(piece, lambda a, b: (b % height, (b // height) * height + a))

    core, ypos, xpos = c & 1, (c >> 1) & 3, c >> 3
    rcore, ry, rx = root_col & 1, (root_col >> 1) & 3, root_col >> 3
    side = lax.broadcasted_iota(jnp.int32, (CHUNK, 2 * NB), 1) < NB
    both = jnp.where(jnp.where(side, core == rcore, core == 1), both, core_twin(both))
    mine = lax.dynamic_slice_in_dim(both, core * HALF, HALF, 0)
    side = side[:HALF]

    def spread(value, position, goal, last, shift):
        source = jnp.where(side, position ^ goal, position ^ last)
        out = value
        for d in range(1, 4):
            out = jnp.where(source == d, send(value, lambda a, b: (a, b ^ (d << shift))), out)
        return out

    mine = spread(mine, xpos, rx, 3, 3)
    piece, mine = tie(piece, mine)
    crossing = double(piece[None], 4)
    mine = spread(mine, ypos, ry, 3, 1)
    moved, crossing, mine = tie(moved, crossing, mine)
    gathered = lax.all_gather(moved, "pcol", axis=0, tiled=False)
    ring = double(double(double(mine[None], 4), 2), 1)
    crossing, ring = tie(crossing, ring)
    facing = send(crossing, lambda a, b: (a ^ 2, b))
    first, carried, rest = first_factor(info, ring, core_twin(ring))
    crossing, facing, carried, rest = tie(crossing, facing, carried, rest)
    crossing = jnp.concatenate([crossing, facing], axis=0)
    beyond = send(crossing, lambda a, b: (a ^ 1, b))
    second, corner = second_factor(carried, rest)
    factors = cross(info, first, second, corner, crossing, beyond)
    panels, trailing = update(info, factors, gathered, flat)
    return panels.reshape(2, br, 1, NB, NB), trailing.reshape(kernel.shape)


def solution(mesh):
    in_specs = (P(None, "prow", None, None, "pcol", None), P())
    out_specs = (P(None, None, "prow", None, None), P(None, "prow", None, None, "pcol", None))
    return jax.shard_map(shards, mesh=mesh, in_specs=in_specs, out_specs=out_specs, check_vma=False)
```

```python
import jax
import jax.numpy as jnp
from jax import lax
from jax.experimental import pallas as pl
from jax.experimental.pallas import tpu as pltpu
from jax.sharding import PartitionSpec as P

BASE = 64
GROUP = 8


def split(v):
    high = v.astype(jnp.bfloat16)
    low = (v - high.astype(jnp.float32)).astype(jnp.bfloat16)
    return high, low


def dot3(a, b, dims=((1,), (0,))):
    (ah, al), (bh, bl) = a, b
    f = lambda u, v: lax.dot_general(u, v, (dims, ((), ())), preferred_element_type=jnp.float32)
    return f(ah, bh) + (f(ah, bl) + f(al, bh))


def stack(b):
    return jnp.concatenate([b[0], b[1], b[0]], axis=0)


def stacked(a, b):
    high, low = split(a)
    return jnp.dot(jnp.concatenate([high, high, low], axis=1), b, preferred_element_type=jnp.float32)


def product(a, b, dims=((1,), (0,))):
    return dot3(split(a), split(b), dims)


def factor_group(scalars):
    n = GROUP
    g = [row[:] for row in scalars]
    unit = [[None] * n for _ in range(n)]
    pivots, inverses = [], []
    for q in range(0, n, 2):
        a, b, d = g[q][q], g[q + 1][q], g[q + 1][q + 1]
        det = a * d - b * b
        over = 1.0 / det
        inv = 1.0 / a
        step = b * inv
        below = d - step * b
        pivots += [a, below]
        inverses += [inv, a * over]
        unit[q + 1][q] = step
        for i in range(q + 2, n):
            x, y = g[i][q], g[i][q + 1]
            unit[i][q] = x * inv
            unit[i][q + 1] = (y * a - x * b) * over
        for i in range(q + 2, n):
            x, y = g[i][q], g[i][q + 1]
            u, v = (x * d - y * b) * over, unit[i][q + 1]
            for k in range(q + 2, i + 1):
                g[i][k] = g[i][k] - (u * g[k][q] + v * g[k][q + 1])
    w = [[None] * n for _ in range(n)]
    for q in range(n):
        for i in range(q + 1, n):
            acc = unit[i][q]
            for k in range(q + 1, i):
                acc = acc + unit[i][k] * w[k][q]
            w[i][q] = -acc
    return w, pivots, inverses


def base_inverse(s):
    lanes = 2 * BASE
    row = lax.broadcasted_iota(jnp.int32, (BASE, BASE), 0)
    col = lax.broadcasted_iota(jnp.int32, (BASE, BASE), 1)
    eye = jnp.where(row == col, 1.0, 0.0).astype(jnp.float32)
    table = jnp.concatenate([s, eye], axis=1)
    groups = [table[GROUP * h : GROUP * h + GROUP, :] for h in range(BASE // GROUP)]
    shape = (GROUP, lanes)
    sub = lax.broadcasted_iota(jnp.int32, shape, 0)
    spread = lambda v: jnp.broadcast_to(v, shape)
    done = []
    for g in range(BASE // GROUP):
        p = groups[g]
        start = GROUP * g
        cols = [spread(p[:, start + q : start + q + 1]) for q in range(GROUP)]
        scalars = [[spread(cols[q][i : i + 1, :]) if i >= q else None for q in range(GROUP)] for i in range(GROUP)]
        w, pivots, inverses = factor_group(scalars)
        rows = [spread(p[q : q + 1, :]) for q in range(GROUP)]
        reduced = []
        for i in range(GROUP):
            acc = rows[i]
            for q in range(i):
                acc = acc + w[i][q] * rows[q]
            reduced.append(acc)
        for h in range(g + 1, BASE // GROUP):
            t = groups[h]
            cb = [spread(t[:, start + q : start + q + 1]) for q in range(GROUP)]
            for q in range(GROUP):
                v = cb[q]
                for k in range(q):
                    v = v + w[q][k] * cb[k]
                t = t - (v * inverses[q]) * reduced[q]
            groups[h] = t
        out = jnp.zeros(shape, jnp.float32)
        for q in range(GROUP):
            out = jnp.where(sub == q, reduced[q] * lax.rsqrt(pivots[q]), out)
        done.append(out)
    return jnp.concatenate(done, axis=0)[:, BASE:]


def pair_inverse(s):
    top = base_inverse(s[:BASE, :BASE])
    below = product(s[BASE:, :BASE], top, ((1,), (1,)))
    rest = s[BASE:, BASE:] - product(below, below, ((1,), (1,)))
    carried = product(below, top)
    bottom = base_inverse(rest)
    corner = -product(bottom, carried)
    return jnp.concatenate(
        [jnp.concatenate([top, jnp.zeros_like(top)], axis=1), jnp.concatenate([corner, bottom], axis=1)], axis=0
    )


def factor_inverse(s_ref, z_ref, m_ref):
    n = s_ref.shape[0]
    size = 2 * BASE
    row = lax.broadcasted_iota(jnp.int32, (n, n), 0)
    col = lax.broadcasted_iota(jnp.int32, (n, n), 1)
    z_ref[...] = jnp.where(row == col, 1.0, 0.0).astype(jnp.float32)

    def step(k, carry):
        here = pl.ds(pl.multiple_of(k * size, size), size)
        inverse = split(pair_inverse(s_ref[here, here]))
        us = split(dot3(inverse, split(s_ref[here, :])))
        uz = dot3(inverse, split(z_ref[here, :]))
        m_ref[here, :] = uz
        uz = split(uz)
        s_ref[...] -= dot3(us, us, ((0,), (0,)))
        z_ref[...] -= dot3(us, uz, ((0,), (0,)))
        return carry

    lax.fori_loop(0, n // size, step, 0)


AXES = ("prow", "pcol")
NB = 256
NEWEST = 63
PLANES = 8
CHUNK = 2 * NB // PLANES
HALF = CHUNK // 2
LANES = 128
VMEM = pl.BlockSpec(memory_space=pltpu.VMEM)
SMEM = pl.BlockSpec(memory_space=pltpu.SMEM)
ROW, COLUMN, ROOT, HELD, FLIPPED, FIRST, SECOND = range(7)
MASKS = (0, 4, 2, 6, 1, 5, 3, 7)
PARAMS = pltpu.CompilerParams(vmem_limit_bytes=48 * 1024 * 1024)


def chunk_of(info, plane):
    return plane // 2 + PLANES // 2 * ((plane + info[ROOT]) % 2)


def place_of(info, plane):
    return (chunk_of(info, plane) + PLANES // 2 * info[FLIPPED]) % PLANES


def block_column(ref, t, rows):
    return jnp.concatenate([ref[pl.ds(2 * t + j, rows, stride=4), :] for j in range(2)], axis=1)


def pick_kernel(info, piece_ref, both_ref):
    both_ref[:, :NB] = block_column(piece_ref, info[HELD], CHUNK)
    both_ref[:, NB:] = block_column(piece_ref, 1, CHUNK)


def pick(info, piece):
    return pl.pallas_call(
        pick_kernel,
        out_shape=jax.ShapeDtypeStruct((CHUNK, 2 * NB), jnp.float32),
        in_specs=[SMEM, VMEM],
        out_specs=VMEM,
        compiler_params=PARAMS,
        name="pick",
    )(info, piece)


def first_kernel(info, own_ref, twin_ref, m_ref, w_ref, rest_ref, d_ref, s_ref, z_ref):
    flip = info[FLIPPED] == 1
    core = info[COLUMN] % 2
    for slot in range(PLANES):
        base = place_of(info, info[ROW] ^ MASKS[slot]) * CHUNK
        for ref, side in ((own_ref, core), (twin_ref, 1 - core)):
            v = ref[slot]
            v = jnp.where(flip, jnp.concatenate([v[:, NB:], v[:, :NB]], axis=1), v)
            d_ref[pl.ds(pl.multiple_of(base + side * HALF, HALF), HALF), :] = v
    s_ref[...] = d_ref[:NB, :NB]
    factor_inverse(s_ref, z_ref, m_ref)
    inverse = split(m_ref[...])
    below = split(dot3(split(d_ref[NB:, :NB]), inverse, ((1,), (1,))))
    rest_ref[...] = d_ref[NB:, NB:] - dot3(below, below, ((1,), (1,)))
    w_ref[...] = dot3(below, inverse)


def second_kernel(info, first_ref, carried_ref, rest_ref, w_ref, t_ref, x_ref, m_ref, s_ref, z_ref):
    s_ref[...] = rest_ref[...]
    factor_inverse(s_ref, z_ref, m_ref)
    t_ref[:NB, :NB] = first_ref[...].T
    t_ref[:NB, NB:] = (-product(m_ref[...], carried_ref[...])).T
    t_ref[NB:, :NB] = jnp.zeros((NB, NB), jnp.float32)
    t_ref[NB:, NB:] = m_ref[...].T
    for plane in range(PLANES):
        start = pl.multiple_of(place_of(info, plane) * CHUNK, CHUNK)
        x_ref[plane * CHUNK : (plane + 1) * CHUNK, :] = t_ref[pl.ds(start, CHUNK), :]
    w_ref[...] = stack(split(x_ref[...]))


def stage(kernel, name, inputs, outputs, scratch):
    return pl.pallas_call(
        kernel,
        out_shape=outputs,
        in_specs=inputs,
        out_specs=[VMEM] * len(outputs),
        scratch_shapes=scratch + [pltpu.VMEM((NB, NB), jnp.float32)] * 2,
        compiler_params=PARAMS,
        cost_estimate=pl.CostEstimate(flops=10**8, transcendentals=0, bytes_accessed=4 * 10**7),
        name=name,
    )


def first_factor(info, own, twin):
    whole = [pltpu.VMEM((2 * NB, 2 * NB), jnp.float32)]
    outputs = [jax.ShapeDtypeStruct((NB, NB), jnp.float32)] * 3
    return stage(first_kernel, "first", [SMEM, VMEM, VMEM], outputs, whole)(info, own, twin)


def second_factor(info, first, carried, rest):
    scratch = [pltpu.VMEM((2 * NB, 2 * NB), jnp.float32)] * 2 + [pltpu.VMEM((NB, NB), jnp.float32)]
    outputs = [jax.ShapeDtypeStruct((6 * NB, 2 * NB), jnp.bfloat16)]
    return stage(second_kernel, "second", [SMEM, VMEM, VMEM, VMEM], outputs, scratch)(info, first, carried, rest)[0]


def cross_kernel(info, w_ref, near_ref, far_ref, c_ref, x_ref):
    n = 2 * NB
    high, low = w_ref[:n].T, w_ref[n : 2 * n].T
    for slot in range(PLANES):
        ref = (near_ref, far_ref)[slot // 4].at[slot % 4]
        start = pl.multiple_of((info[ROW] ^ MASKS[slot]) * CHUNK, CHUNK)
        for column in range(2):
            x_ref[pl.ds(start, CHUNK), column * NB : (column + 1) * NB] = block_column(ref, column, CHUNK)
    rows = jnp.concatenate([high, high, low], axis=1)
    c_ref[...] = stack(split(jnp.dot(rows, stack(split(x_ref[...])), preferred_element_type=jnp.float32)))


def cross(info, weights, near, far):
    n = 2 * NB
    return pl.pallas_call(
        cross_kernel,
        out_shape=jax.ShapeDtypeStruct((3 * n, n), jnp.bfloat16),
        in_specs=[SMEM] + [VMEM] * 3,
        out_specs=VMEM,
        scratch_shapes=[pltpu.VMEM((n, n), jnp.float32)],
        compiler_params=PARAMS,
        name="cross",
    )(info, weights, near, far)


def update_kernel(info, w_ref, c_ref, g_ref, a_ref, panels_ref, t_ref):
    group = pl.program_id(0)
    first, second = info[FIRST], info[SECOND]
    for t in range(2):
        block = (t * pl.num_programs(0) + group) * PLANES + info[ROW]
        columns = jnp.concatenate([block_column(g_ref.at[plane], t, CHUNK) for plane in range(PLANES)], axis=0)
        rows = stacked(columns.T, w_ref[...])
        row_kept = (block != first) & (block != second)
        panels_ref[0, t, 0] = rows[:, :NB]
        panels_ref[1, t, 0] = jnp.where(block != first, rows[:, NB:], 0.0)
        trail = stacked(rows, c_ref[...])
        for column in range(2):
            number = info[COLUMN] + 32 * column
            kept = row_kept & (number != first) & (number != second)
            for j in range(2):
                where = pl.ds(2 * column + j, NB, stride=4)
                start = column * NB + j * LANES
                t_ref[t, 0, where, :] = jnp.where(kept, a_ref[t, 0, where, :] - trail[:, start : start + LANES], 0.0)


def update(info, factors, gathered, flat):
    br, rows, _ = flat.shape
    groups = gathered.shape[0] // PLANES
    block = lambda k, info: (0, k, 0, 0)
    return pl.pallas_call(
        update_kernel,
        grid_spec=pltpu.PrefetchScalarGridSpec(
            num_scalar_prefetch=1,
            grid=(groups,),
            in_specs=[VMEM] * 2
            + [
                pl.BlockSpec((PLANES, 4 * CHUNK, LANES), lambda k, info: (k, 0, 0)),
                pl.BlockSpec((2, 1, rows, LANES), block),
            ],
            out_specs=[
                pl.BlockSpec((2, 2, 1, NB, NB), lambda k, info: (0, 0, k, 0, 0)),
                pl.BlockSpec((2, 1, rows, LANES), block),
            ],
        ),
        out_shape=[
            jax.ShapeDtypeStruct((2, 2, groups, NB, NB), jnp.float32),
            jax.ShapeDtypeStruct((2, groups) + flat.shape[1:], jnp.float32),
        ],
        compiler_params=PARAMS,
        name="update",
    )(info, *factors, gathered, flat.reshape((2, groups) + flat.shape[1:]))


def shards(kernel, pivots):
    height, width = lax.axis_size("prow"), lax.axis_size("pcol")
    assert (height, width) == (PLANES, 32)
    br, bc = kernel.shape[0], kernel.shape[3]
    assert bc == 2
    flat = kernel.reshape(br, NB * bc * NB // LANES, LANES)
    r = lax.axis_index("prow")
    c = lax.axis_index("pcol")
    flipped = pivots[0] == NEWEST
    other = jnp.where(flipped, pivots[1], pivots[0])
    block_row, root_row = other >> 3, other & 7
    root_t, root_col = other >> 5, other & 31
    info = jnp.stack([r, c, root_row, root_t, flipped.astype(jnp.int32), pivots[0], pivots[1]])
    device = lambda row, column: row * width + column
    everyone = [(row, column) for row in range(height) for column in range(width)]
    send = lambda value, to: lax.ppermute(value, AXES, [(device(a, b), device(*to(a, b))) for a, b in everyone])
    double = lambda value, mask: jnp.concatenate([value, send(value, lambda a, b: (a ^ mask, b))], axis=0)
    tie = lambda *values: lax.optimization_barrier(values)
    core_twin = lambda value: send(value, lambda a, b: (a, b ^ 1))

    piece_rows = 4 * CHUNK
    part = lambda rows, q: rows[q * piece_rows : (q + 1) * piece_rows]
    line = lambda start, end: [(device(start, k), device(end, k)) for k in range(width)]

    def scatter_from(root):
        parity, quarter = root % 2, root // 2
        away = 1 - parity

        def run(others, newest):
            arrived = []
            for q in range(4):
                plane = 2 * q + away
                if plane != height - 1:
                    arrived.append((plane, lax.ppermute(part(newest, q), AXES, line(height - 1, plane))))
                if q != quarter:
                    plane = 2 * q + parity
                    pairs = line(root, plane)
                    if quarter in (1, 2):
                        pairs = line(2 * quarter, 2 * q) + line(2 * quarter + 1, 2 * q + 1)
                    arrived.append((plane, lax.ppermute(part(others, q), AXES, pairs)))
            arrived.append((root, part(others, quarter)))
            if away == 1:
                arrived.append((height - 1, part(newest, 3)))
            piece = arrived[0][1]
            for plane, value in arrived[1:]:
                piece = jnp.where(r == plane, value, piece)
            return piece

        return run

    others = lax.dynamic_slice(flat, (block_row, 0, 0), (1,) + flat.shape[1:])[0]
    rows = tie(others, flat[NEWEST // height])
    piece = lax.switch(root_row, [scatter_from(root) for root in range(height)], *rows)
    both = pick(info, piece)

    moved = send(piece, lambda a, b: (b % height, (b // height) * height + a))

    core, ypos, xpos = c & 1, (c >> 1) & 3, c >> 3
    rcore, ry, rx = root_col & 1, (root_col >> 1) & 3, root_col >> 3
    side = lax.broadcasted_iota(jnp.int32, (CHUNK, 2 * NB), 1) < NB
    both = jnp.where(jnp.where(side, core == rcore, core == 1), both, core_twin(both))
    mine = lax.dynamic_slice_in_dim(both, core * HALF, HALF, 0)
    side = side[:HALF]

    def spread(value, position, goal, last, shift):
        source = jnp.where(side, position ^ goal, position ^ last)
        out = value
        for d in range(1, 4):
            out = jnp.where(source == d, send(value, lambda a, b: (a, b ^ (d << shift))), out)
        return out

    mine = spread(mine, xpos, rx, 3, 3)
    piece, mine = tie(piece, mine)
    crossing = double(piece[None], 4)
    mine = spread(mine, ypos, ry, 3, 1)
    moved, crossing, mine = tie(moved, crossing, mine)
    gathered = lax.all_gather(moved, "pcol", axis=0, tiled=False)
    ring = double(double(double(mine[None], 4), 2), 1)
    crossing, ring = tie(crossing, ring)
    facing = send(crossing, lambda a, b: (a ^ 2, b))
    first, carried, rest = first_factor(info, ring, core_twin(ring))
    crossing, facing, carried, rest = tie(crossing, facing, carried, rest)
    crossing = jnp.concatenate([crossing, facing], axis=0)
    beyond = send(crossing, lambda a, b: (a ^ 1, b))
    weights = second_factor(info, first, carried, rest)
    factors = weights, cross(info, weights, crossing, beyond)
    panels, trailing = update(info, factors, gathered, flat)
    return panels.reshape(2, br, 1, NB, NB), trailing.reshape(kernel.shape)


def solution(mesh):
    in_specs = (P(None, "prow", None, None, "pcol", None), P())
    out_specs = (P(None, None, "prow", None, None), P(None, "prow", None, None, "pcol", None))
    return jax.shard_map(shards, mesh=mesh, in_specs=in_specs, out_specs=out_specs, check_vma=False)
```
